512 devices in a mesh: dp: 16 (over x, y), expert: 32 (over z, core).
Axes of the slice: x: 4, y: 4, z: 16, core: 2. Of those that a mesh axis runs over, the one named last changes fastest.
Arguments:
- tokens: bfloat16 [1024, 4096], P('expert', 'dp'), may hold values from -6 to 6
- expert_ids: int32 [1024, 8], P('expert'), may hold values from 0 to 31, all different within a row; in each aligned block of 32 rows (0 to 31, 32 to 63, ...) at most 16 rows name the same one
- route_weights: float32 [1024, 8], P('expert'), may hold values from 0.1 to 1
- gate_weight: bfloat16 [32, 1536, 4096], P('expert', None, 'dp'), may hold values from -0.09375 to 0.09375
- up_weight: bfloat16 [32, 1536, 4096], P('expert', None, 'dp'), may hold values from -0.09375 to 0.09375
- down_weight: bfloat16 [32, 1536, 4096], P('expert', None, 'dp'), may hold values from -0.15625 to 0.15625
- output_grad: bfloat16 [1024, 4096], P('expert', 'dp'), may hold values from -1.5 to 1.5
Outputs:
- layer_output: bfloat16 [1024, 4096], P('expert', 'dp')
- token_gradient: bfloat16 [1024, 4096], P('expert', 'dp')
- route_gradient: float32 [1024, 8], P('expert')
- gate_gradient: bfloat16 [32, 1536, 4096], P('expert', None, 'dp')
- up_gradient: bfloat16 [32, 1536, 4096], P('expert', None, 'dp')
- down_gradient: bfloat16 [32, 1536, 4096], P('expert', None, 'dp')
The draws below stay inside these ranges and needn't reach their ends.
Inputs may be any that keep to these rules, and one draw needn't show every extreme that they name: `expert_ids`: within each aligned block of 32 tokens no expert is named more than 16 times, and in every draw some block names some expert exactly 16 times; the experts of one token differ.
All inputs are finite; a program needn't handle non-finite values.
Results may differ from the reference program's by a relative error of at most 0.023.
Values may be sent and summed in bfloat16 or wider, within the bound.
A program may use at most 64 MiB of HBM per device.

```python
import math
import jax
import jax.numpy as jnp
import numpy as np
from jax import lax

D = 4096
HID = 1536
TOP = 8
TOK = 32
EXPERTS = 32
CAP = 16
TOKENS = 1024
N_DP = 16
N_EXPERT = 32


def levels(stream_key, dims, pieces, smallest, top_value):
    def one(dim, parts):
        heights = jax.random.uniform(jax.random.fold_in(jax.random.fold_in(stream_key, 6), dim), (parts,), jnp.float32, smallest / len(pieces), top_value / len(pieces))
        return jnp.repeat(jnp.exp(heights), dims[dim] // parts).reshape((-1,) + (1,) * (len(dims) - dim - 1))

    factor_of = one(*pieces[0])
    for cut in pieces[1:]:
        factor_of = factor_of * one(*cut)
    return factor_of


def assign_block(stream_key, own, number, rows, number_of, top, bound, slope):
    ranking = jax.random.permutation(stream_key, number_of)
    heavy_load, ordinary = shares(number_of, rows * top, bound, slope, True), shares(number_of, rows * top, bound, slope, False)
    places = jnp.arange(number_of)

    def named(lengths, turn):
        used = int((lengths > 0).sum())
        fixed = max(1, used // 4)
        shifted = fixed + (places - fixed + turn * (used - fixed)) % max(1, number_of - fixed)
        return jnp.zeros((number_of,), jnp.int32).at[ranking[jnp.where(places < fixed, places, shifted)]].set(jnp.asarray(lengths, jnp.int32))

    lengths = jnp.where(number % 4 == 0, named(heavy_load, number // 4), named(ordinary, number - number // 4 - 1))
    mixed = jax.random.permutation(jax.random.fold_in(own, 3), number_of)
    source_of, taker = mixed[0:number_of // 2 * 2:2], mixed[1:number_of // 2 * 2:2]
    margin = jnp.minimum(lengths[source_of] - 1, bound - lengths[taker]) // 2
    margin = jnp.where((source_of == ranking[0]) | (taker == ranking[0]) | (lengths[taker] == 0), 0, jnp.maximum(margin, 0))
    shifted = jax.random.randint(jax.random.fold_in(own, 4), (number_of // 2,), 0, 1 << 20) % (margin + 1)
    lengths = lengths.at[source_of].add(-shifted).at[taker].add(shifted)
    labels = jnp.searchsorted(jnp.cumsum(lengths), jnp.arange(rows * top), side="right").astype(jnp.int32)
    grid = labels.reshape(top, rows).T
    grid = grid[jax.random.permutation(jax.random.fold_in(own, 1), rows)]
    turn = jax.random.randint(jax.random.fold_in(own, 2), (rows, 1), 0, top)
    return jnp.take_along_axis(grid, (jnp.arange(top)[None, :] + turn) % top, axis=1)


def shares(count, total, most, lean, full):
    portions = [(1 << 20) // math.isqrt(rank ** lean) + 1 for rank in range(1, count + 1)]
    largest = most if full else min(most, max(-(-total // count), total * portions[0] // sum(portions)))
    least = 1 if total - largest >= count - 1 else 0
    given, spare = [largest] + [least] * (count - 1), total - largest - least * (count - 1)
    while spare > 0:
        free = [i for i in range(1, count) if given[i] < largest] or [i for i in range(1, count) if given[i] < most]
        whole, remaining = sum([portions[i] for i in free]), spare
        for i in free:
            addition = min(most - given[i], max(1, remaining * portions[i] // whole), spare)
            given[i] = given[i] + addition
            spare = spare - addition
    return np.array(given)


def normal_values(own_key, extent, deviation, limit, shards=(), kind=jnp.bfloat16):
    array = deviation * jax.random.normal(own_key, extent, jnp.float32)
    if shards:
        array = array * levels(own_key, extent, shards, -0.22, 0.18)
    return jnp.clip(array, -limit, limit).astype(kind)


def setup_inputs(seed: int = 0) -> dict:
    seeds = jax.random.split(jax.random.key(seed), 8)
    tokens = normal_values(seeds[0], (TOKENS, D), 1.0, 6.0, ((0, 32), (1, 16)))
    expert_ids_keys = jax.random.split(jax.random.fold_in(seeds[1], 1), TOKENS // TOK)
    expert_ids_turns = jax.random.permutation(jax.random.fold_in(seeds[1], 3), TOKENS // TOK)
    expert_ids = jax.vmap(lambda own, number: assign_block(jax.random.fold_in(seeds[1], 2), own, number, TOK, EXPERTS, TOP, CAP, 2))(expert_ids_keys, expert_ids_turns).reshape((TOKENS, TOP))
    route_weights = jnp.clip(0.1 + 0.9 * jax.random.uniform(seeds[2], (TOKENS, TOP), jnp.float32) ** levels(seeds[2], (TOKENS, TOP), ((0, 32),), -0.2, 0.2), 0.1, 1.0)
    gate_weight = normal_values(seeds[3], (EXPERTS, HID, D), D ** -0.5, 0.09375, ((0, 32), (2, 16)))
    up_weight = normal_values(seeds[4], (EXPERTS, HID, D), D ** -0.5, 0.09375, ((0, 32), (2, 16)))
    down_weight = normal_values(seeds[5], (EXPERTS, HID, D), HID ** -0.5, 0.15625, ((0, 32), (2, 16)))
    output_grad = normal_values(seeds[6], (TOKENS, D), 0.25, 1.5, ((0, 32), (1, 16)))
    return {"tokens": tokens, "expert_ids": expert_ids, "route_weights": route_weights, "gate_weight": gate_weight, "up_weight": up_weight, "down_weight": down_weight, "output_grad": output_grad}


highest = lax.Precision.HIGHEST


def slot_tables(expert_ids):
    blocks = expert_ids.reshape(N_EXPERT, TOK * TOP)
    member = (blocks[:, :, None] == jnp.arange(EXPERTS, dtype=jnp.int32)[None, None, :]).astype(jnp.int32)
    before = jnp.cumsum(member, axis=1) - member
    rank_in = jnp.sum(before * member, axis=2)
    slot_ids = blocks * CAP + rank_in
    table = slot_ids[:, :, None] == jnp.arange(EXPERTS * CAP, dtype=jnp.int32)[None, None, :]
    return table.reshape(N_EXPERT, TOK, TOP, EXPERTS * CAP).astype(jnp.float32)


def block_sum(row_block, matrix):
    row_count = row_block.shape[0]
    width = D // N_DP
    rows = row_block.astype(jnp.float32).reshape(row_count, N_DP, width).transpose(1, 0, 2)
    cols = matrix.astype(jnp.float32).reshape(HID, N_DP, width).transpose(1, 0, 2)
    terms = jnp.einsum('srd,shd->srh', rows, cols, precision=highest)
    held = lax.optimization_barrier(terms.astype(jnp.bfloat16))
    return jnp.sum(held.astype(jnp.float32), axis=0)


def to_experts(spread, row_block):
    buffer = jnp.einsum('bts,btd->bsd', spread, row_block, precision=highest).astype(jnp.bfloat16)
    buffer = buffer.reshape(N_EXPERT, EXPERTS, CAP, D).transpose(1, 0, 2, 3)
    return buffer.reshape(EXPERTS, N_EXPERT * CAP, D)


def from_experts(row_block):
    row_block = row_block.reshape(EXPERTS, N_EXPERT, CAP, D).transpose(1, 0, 2, 3)
    return row_block.reshape(N_EXPERT, EXPERTS * CAP, D).astype(jnp.float32)


def expert_pass(operands):
    row_block, grad_block, gate_matrix, up_matrix, down_matrix = operands
    gate_pre = block_sum(row_block, gate_matrix)
    up_pre = block_sum(row_block, up_matrix)
    sigmoid_gate = jax.nn.sigmoid(gate_pre)
    silu_gate = gate_pre * sigmoid_gate
    hidden_act = (silu_gate * up_pre).astype(jnp.bfloat16)
    expert_out = jnp.dot(hidden_act, down_matrix, preferred_element_type=jnp.float32).astype(jnp.bfloat16)
    hidden_grad = block_sum(grad_block, down_matrix)
    silu_slope = sigmoid_gate * (1.0 + gate_pre * (1.0 - sigmoid_gate))
    gate_delta = (hidden_grad * up_pre * silu_slope).astype(jnp.bfloat16)
    up_delta = (hidden_grad * silu_gate).astype(jnp.bfloat16)
    down_gradient = jnp.dot(hidden_act.T, grad_block, preferred_element_type=jnp.float32).astype(jnp.bfloat16)
    gate_gradient = jnp.dot(gate_delta.T, row_block, preferred_element_type=jnp.float32).astype(jnp.bfloat16)
    up_gradient = jnp.dot(up_delta.T, row_block, preferred_element_type=jnp.float32).astype(jnp.bfloat16)
    back_out = jnp.dot(gate_delta, gate_matrix, preferred_element_type=jnp.float32)
    back_out = back_out + jnp.dot(up_delta, up_matrix, preferred_element_type=jnp.float32)
    back_out = back_out.astype(jnp.bfloat16)
    return expert_out, back_out, gate_gradient, up_gradient, down_gradient


def reference(tokens, expert_ids, route_weights, gate_weight, up_weight, down_weight, output_grad):
    table = slot_tables(expert_ids)
    picked = jnp.sum(table, axis=2)
    weights = route_weights.reshape(N_EXPERT, TOK, TOP)
    weighted = jnp.sum(table * weights[:, :, :, None], axis=2)
    dispatched = to_experts(picked, tokens.reshape(N_EXPERT, TOK, D).astype(jnp.float32))
    grads = output_grad.reshape(N_EXPERT, TOK, D).astype(jnp.float32)
    grad_dispatched = to_experts(weighted, grads)
    results = lax.map(expert_pass, (dispatched, grad_dispatched, gate_weight, up_weight, down_weight))
    expert_out, back_out, gate_gradient, up_gradient, down_gradient = results
    returned = from_experts(expert_out)
    layer_output = jnp.einsum('bts,bsd->btd', weighted, returned, precision=highest)
    layer_output = layer_output.astype(jnp.bfloat16).reshape(TOKENS, D)
    slot_grad = jnp.einsum('btd,bsd->bts', grads, returned, precision=highest)
    route_gradient = jnp.sum(table * slot_grad[:, :, None, :], axis=3).reshape(TOKENS, TOP)
    back_rows = from_experts(back_out)
    token_gradient = jnp.einsum('bts,bsd->btd', picked, back_rows, precision=highest)
    token_gradient = token_gradient.astype(jnp.bfloat16).reshape(TOKENS, D)
    return (layer_output, token_gradient, route_gradient, gate_gradient, up_gradient, down_gradient)
```

```python
import jax
import jax.numpy as jnp
from jax import lax
from jax.experimental import pallas as pl
from jax.experimental.pallas import tpu as pltpu
from jax.sharding import PartitionSpec as P

MESH = pl.DeviceIdType.MESH
BF = jnp.bfloat16
F32 = jnp.float32

WAVES = ((0, 15, 1, 14), (2, 13, 3, 12), (4, 11, 5, 10), (6, 9, 7, 8))
NZ = 16
NW = 4
LAG = 2
STAGES = 9


def dot_last(a, b):
    return lax.dot_general(a, b, (((1,), (1,)), ((), ())), preferred_element_type=F32)


def dot_first(a, b):
    return lax.dot_general(a, b, (((0,), (0,)), ((), ())), preferred_element_type=F32)


def dot_plain(a, b):
    return lax.dot_general(a, b, (((1,), (0,)), ((), ())), preferred_element_type=F32)


def kernel(
    tok, ids, rw, og, wg, wu, wd,
    lo_out, tg_out, rg_out, gg, ug, dg,
    W, G, X, GD, WC, S, M1P, M1M, RP, RM, Q1P, Q1M, QP, QM, A, H3, RET, RR, OUT,
    w_sem, o_sem, z_snd, z_rcv, b_snd, b_rcv, s_snd, s_rcv, a_snd, a_rcv, t_snd, t_rcv,
):
    dp = lax.axis_index("dp")
    e = lax.axis_index("expert")
    x, y = dp // 4, dp % 4
    z, c = e // 2, e % 2
    pos = (x, y)

    def along(axis, step):
        if axis == 0:
            return {"dp": lax.rem(x + step, 4) * 4 + y}
        return {"dp": x * 4 + lax.rem(y + step, 4)}

    def on_z(step, other):
        return {"expert": lax.rem(z + step, NZ) * 2 + ((1 - c) if other else c)}

    loads = [
        pltpu.make_async_copy(src, W.at[n], w_sem.at[n]) for n, src in enumerate((wg, wu, wd))
    ]
    for load in loads:
        load.start()

    barrier = pltpu.get_barrier_semaphore()
    for axis in (0, 1):
        for step in (1, 3):
            pl.semaphore_signal(barrier, inc=1, device_id=along(axis, step), device_id_type=MESH)

    def greet(d, carry):
        pl.semaphore_signal(
            barrier, inc=1, device_id={"expert": lax.rem(e + d, 2 * NZ)}, device_id_type=MESH
        )
        return carry

    lax.fori_loop(1, 2 * NZ, greet, 0)

    lane = lax.broadcasted_iota(jnp.int32, (32, 128), 1)
    ex = lane % 32
    dense = jnp.zeros((32, 128), F32)
    member = jnp.zeros((32, 128), F32)
    for k in range(8):
        hit = ex == ids[:, k : k + 1]
        dense = dense + jnp.where(hit, rw[:, k : k + 1], 0.0)
        member = member + jnp.where(hit, 1.0, 0.0)
    tri = lax.broadcasted_iota(jnp.int32, (32, 32), 1) < lax.broadcasted_iota(jnp.int32, (32, 32), 0)
    before = dot_plain(jnp.where(tri, 1.0, 0.0).astype(BF), member.astype(BF))
    code = member * (before + 1.0)
    hi = dense.astype(BF)
    rest = dense - hi.astype(F32)
    mid = rest.astype(BF)
    low = (rest - mid.astype(F32)).astype(BF)
    meta = jnp.where(
        lane < 32,
        code,
        jnp.where(lane < 64, hi.astype(F32), jnp.where(lane < 96, mid.astype(F32), low.astype(F32))),
    )
    G[0, 0, :, 0:256] = tok[...]
    G[0, 0, :, 256:512] = og[...]
    G[0, 0, :, 512:640] = meta.astype(BF)

    pl.semaphore_wait(barrier, 2 * NZ - 1 + 4)

    sent = []

    def send(src, dst, snd, rcv, to):
        copy = pltpu.make_async_remote_copy(
            src_ref=src, dst_ref=dst, send_sem=snd, recv_sem=rcv, device_id=to, device_id_type=MESH
        )
        copy.start()
        sent.append(copy)
        return copy

    ring = {}

    def ring_send(s):
        ring[0, s] = send(
            G.at[0, (1 - s) % NZ], G.at[0, (-s) % NZ], z_snd.at[0, s], z_rcv.at[0, s], on_z(1, False)
        )
        if s < 8:
            ring[1, s] = send(
                G.at[0, s - 1], G.at[0, s], z_snd.at[1, s], z_rcv.at[1, s], on_z(NZ - 1, False)
            )

    def sib_send(r):
        ring["s", r] = send(G.at[0, r], G.at[1, r], b_snd.at[r], b_rcv.at[r], on_z(0, True))

    pumped = [0]

    def pump(upto):
        while pumped[0] < min(upto, 8):
            pumped[0] += 1
            s = pumped[0]
            ring[0, s].wait_recv()
            if s < 8:
                ring[1, s].wait_recv()
                ring_send(s + 1)
            sib_send((-s) % NZ)
            if s < 8:
                sib_send(s)

    ring_send(1)
    sib_send(0)

    made = {}

    def ring_pair(key, fwd, back, axis):
        for n, (src, dst) in enumerate(fwd):
            made[key, 0, n] = send(src, dst, *sems(key, 0, n), along(axis, 1))
        for n, (src, dst) in enumerate(back):
            made[key, 1, n] = send(src, dst, *sems(key, 1, n), along(axis, 3))

    def sems(key, d, n):
        kind, w, h, ph = key
        if kind == "s":
            return s_snd.at[w, h, ph, d, n], s_rcv.at[w, h, ph, d, n]
        return a_snd.at[w, h, ph, d, n], a_rcv.at[w, h, ph, d, n]

    def arrived(key, d, n):
        made[key, d, n].wait_recv()

    def reduce_start(w, h, ph):
        axis = h if ph == 0 else 1 - h
        i = pos[axis]
        if ph == 0:
            part = lambda t, us: S.at[w, h, t, :, us]
            m1p, m1m, rp, rm = M1P.at[w, h], M1M.at[w, h], RP, RM
            into = lambda r, us: r.at[w, h, :, us]
        else:
            own = pos[h]
            part = lambda t, us: S.at[w, h, own, t, us]
            m1p, m1m, rp, rm = Q1P.at[w, h], Q1M.at[w, h], QP, QM
            into = lambda r, us: r.at[w, h, us]
        L, R = pl.ds(0, 5), pl.ds(5, 4)
        two, nxt, prv = lax.rem(i + 2, 4), lax.rem(i + 1, 4), lax.rem(i + 3, 4)
        ring_pair(
            ("s", w, h, ph),
            ((part(two, L), m1p), (part(nxt, R), into(rp, R))),
            ((part(two, R), m1m), (part(prv, L), into(rm, L))),
            axis,
        )

    def reduce_merge(w, h, ph):
        axis = h if ph == 0 else 1 - h
        i = pos[axis]
        key = ("s", w, h, ph)
        nxt, prv = lax.rem(i + 1, 4), lax.rem(i + 3, 4)
        L, R = pl.ds(0, 5), pl.ds(5, 4)
        if ph == 0:
            part = lambda t, us: S.at[w, h, t, :, us]
            m1p, m1m, rp, rm = M1P.at[w, h], M1M.at[w, h], RP, RM
            into = lambda r, us: r.at[w, h, :, us]
        else:
            own = pos[h]
            part = lambda t, us: S.at[w, h, own, t, us]
            m1p, m1m, rp, rm = Q1P.at[w, h], Q1M.at[w, h], QP, QM
            into = lambda r, us: r.at[w, h, us]
        for d, tgt, us, m1, r in ((0, nxt, L, m1p, rp), (1, prv, R, m1m, rm)):
            arrived(key, d, 0)
            ref = part(tgt, us)
            ref[...] = (ref[...].astype(F32) + m1[...].astype(F32)).astype(BF)
            made[key, d, 2] = send(ref, into(r, us), *sems(key, d, 2), along(axis, 1 if d == 0 else 3))

    def reduce_end(w, h, ph):
        key = ("s", w, h, ph)
        for d in (0, 1):
            arrived(key, d, 1)
            arrived(key, d, 2)
        if ph == 0:
            i = pos[h]
            total = S[w, h, i].astype(F32) + RP[w, h].astype(F32) + RM[w, h].astype(F32)
            S[w, h, i] = total.astype(BF)
            return None
        return S[w, h, pos[h], pos[1 - h]].astype(F32) + QP[w, h].astype(F32) + QM[w, h].astype(F32)

    def gather_start(w, h, ph):
        axis = 1 - h if ph == 0 else h
        i, j = pos[h], pos[1 - h]
        L, R = pl.ds(0, 5), pl.ds(5, 5 - h)
        part = (lambda us: A.at[w, h, i, j, us]) if ph == 0 else (lambda us: A.at[w, h, i, :, us])
        ring_pair(
            ("a", w, h, ph),
            ((part(L), part(L)), (part(R), part(R))),
            ((part(R), part(R)), (part(L), part(L))),
            axis,
        )

    def gather_forward(w, h, ph):
        axis = 1 - h if ph == 0 else h
        key = ("a", w, h, ph)
        i, j = pos[h], pos[1 - h]
        nxt, prv = lax.rem(pos[axis] + 1, 4), lax.rem(pos[axis] + 3, 4)
        L, R = pl.ds(0, 5), pl.ds(5, 5 - h)
        for d, src, us in ((0, prv, L), (1, nxt, R)):
            arrived(key, d, 0)
            ref = A.at[w, h, i, src, us] if ph == 0 else A.at[w, h, src, :, us]
            made[key, d, 2] = send(ref, ref, *sems(key, d, 2), along(axis, 1 if d == 0 else 3))

    def gather_end(w, h, ph):
        for d in (0, 1):
            arrived(("a", w, h, ph), d, 1)
            arrived(("a", w, h, ph), d, 2)

    def partials(w):
        blocks = [(r, o) for r in WAVES[w] for o in (0, 1)]
        pump(max(min(r, NZ - r) for r in WAVES[w]))
        for r in WAVES[w]:
            ring["s", r].wait_recv()
        tokens = jnp.concatenate([G[o, r, :, 0:256] for r, o in blocks], axis=0)
        grads = jnp.concatenate([G[o, r, :, 256:512] for r, o in blocks], axis=0)
        info_in = jnp.concatenate([G[o, r, :, 512:640] for r, o in blocks], axis=0)
        row = lax.broadcasted_iota(jnp.int32, (16, 128), 0)
        col = lax.broadcasted_iota(jnp.int32, (16, 128), 1)
        pick = jnp.where((col == row * 32 + e) & (row < 4), 1.0, 0.0).astype(BF)
        info = dot_last(pick, info_in)
        w_row = info[1:2] + info[2:3] + info[3:4]
        s_i = lax.broadcasted_iota(jnp.int32, (128, 256), 0)
        t_i = lax.broadcasted_iota(jnp.int32, (128, 256), 1)
        sel = (s_i // 16 == t_i // 32) & (info[0:1] == (s_i % 16 + 1).astype(F32))
        sel_b = jnp.where(sel, 1.0, 0.0).astype(BF)
        w_col = jnp.sum(jnp.where(sel, w_row, 0.0), axis=1, keepdims=True)
        rows = dot_plain(sel_b, tokens).astype(BF)
        rows_g = (dot_plain(sel_b, grads) * w_col).astype(BF)
        X[w] = rows
        GD[w] = rows_g
        WC[w] = jnp.broadcast_to(w_col, (128, 128)).reshape(8, 16, 128)
        for t in range(3):
            if w == 0:
                loads[t].wait()
            src = rows if t < 2 else rows_g
            for n in range(6):
                out = dot_last(src, W[t, n * 256 : (n + 1) * 256, :]).astype(BF)
                q = n // 3
                for part in (0, 1):
                    k = (n % 3) * 2 + part
                    h, u = k // 3, (k % 3) * 3 + t
                    for j in range(8):
                        tile = out[16 * j : 16 * j + 16, part * 128 : part * 128 + 128]
                        if h == 0:
                            S[w, 0, j // 2, 2 * (j % 2) + q, u] = tile
                        else:
                            S[w, 1, 2 * (j % 2) + q, j // 2, u] = tile
        for h in (0, 1):
            reduce_start(w, h, 0)

    def nonlinear(w):
        rg = jnp.zeros((16, 1), F32)
        for h in (0, 1):
            total = reduce_end(w, h, 1)
            i, j = pos[h], pos[1 - h]
            for k in range(3):
                gate, up, hid = total[3 * k], total[3 * k + 1], total[3 * k + 2]
                sig = jax.nn.sigmoid(gate)
                silu = gate * sig
                act = (silu * up).astype(BF)
                A[w, h, i, j, 3 * k] = act
                A[w, h, i, j, 3 * k + 1] = (hid * up * (sig * (1.0 + gate * (1.0 - sig)))).astype(BF)
                A[w, h, i, j, 3 * k + 2] = (hid * silu).astype(BF)
                rg = rg + jnp.sum(act.astype(F32) * hid, axis=1, keepdims=True)
        wc = WC[w, 2 * x + y // 2]
        used = wc > 0.0
        rg = jnp.where(used, rg / jnp.where(used, wc, 1.0), 0.0)
        A[w, 0, x, y, 9] = in_two(rg)
        for h in (0, 1):
            gather_start(w, h, 0)

    lane16 = lax.broadcasted_iota(jnp.int32, (16, 128), 1)

    def in_two(v):
        top = v.astype(BF).astype(F32)
        return jnp.where(lane16 < 64, top, v - top).astype(BF)

    back = {}

    def results(w):
        for h in (0, 1):
            gather_end(w, h, 1)
        base = w * 128
        for j in range(8):
            for q in (0, 1):
                for h in (0, 1):
                    for k in range(3):
                        for t in range(3):
                            if h == 0:
                                tile = A[w, 0, j // 2, 2 * (j % 2) + q, 3 * k + t]
                            else:
                                tile = A[w, 1, 2 * (j % 2) + q, j // 2, 3 * k + t]
                            at = q * 768 + (h * 3 + k) * 128
                            H3[t, base + 16 * j : base + 16 * j + 16, at : at + 128] = tile
        eo = dot_plain(H3[0, base : base + 128, :], W[2]).astype(BF)
        bo = dot_plain(H3[1, base : base + 128, :], W[0])
        bo = (bo + dot_plain(H3[2, base : base + 128, :], W[1])).astype(BF)
        for j in range(8):
            r, o = WAVES[w][j // 2], j % 2
            v = A[w, 0, j // 2, 2 * o, 9].astype(F32) + A[w, 0, j // 2, 2 * o + 1, 9].astype(F32)
            v = in_two(v + pltpu.roll(v, 64, 1))
            local = r == 0 and o == 0
            to = RR.at[0, 0] if local else RET.at[w, j]
            to[:, 0:256] = eo[16 * j : 16 * j + 16]
            to[:, 256:512] = bo[16 * j : 16 * j + 16]
            to[:, 512:640] = v
            if not local:
                m = (NZ - r) % NZ
                back[o, m] = send(
                    RET.at[w, j], RR.at[o, m], t_snd.at[o, m], t_rcv.at[o, m], on_z(r, o == 1)
                )

    def stage(k, w):
        if k == 0:
            partials(w)
        elif k == 4:
            nonlinear(w)
        elif k == 8:
            results(w)
        else:
            for h in (0, 1):
                if k == 1:
                    reduce_merge(w, h, 0)
                elif k == 2:
                    reduce_end(w, h, 0)
                    reduce_start(w, h, 1)
                elif k == 3:
                    reduce_merge(w, h, 1)
                elif k == 5:
                    gather_forward(w, h, 0)
                elif k == 6:
                    gather_end(w, h, 0)
                    gather_start(w, h, 1)
                elif k == 7:
                    gather_forward(w, h, 1)

    for tick in range(STAGES + LAG * (NW - 1)):
        pump(2 + 2 * tick)
        for w in range(NW):
            k = tick - LAG * w
            if 0 <= k < STAGES:
                stage(k, w)

    rows_x = X[...].reshape(512, 256)
    rows_g = GD[...].reshape(512, 256)
    stores = []
    for t, (n_h, rhs, dst) in enumerate(((1, rows_x, gg), (2, rows_x, ug), (0, rows_g, dg))):
        for n in range(6):
            cols = H3[n_h, :, n * 256 : (n + 1) * 256]
            OUT[t, n * 256 : (n + 1) * 256, :] = dot_first(cols, rhs).astype(BF)
        store = pltpu.make_async_copy(OUT.at[t], dst, o_sem.at[t])
        store.start()
        stores.append(store)

    s_i = lax.broadcasted_iota(jnp.int32, (128, 512), 1)
    l_i = lax.broadcasted_iota(jnp.int32, (128, 512), 0)

    def expert_of(s):
        blk = s // 16
        core = jnp.where(blk < NZ, c, 1 - c)
        return (z + blk % NZ) % NZ * 2 + core

    e_s = expert_of(s_i)
    pick_code = jnp.where(l_i == e_s, 1.0, 0.0).astype(BF)
    pick_w = jnp.where((l_i >= 32) & (l_i % 32 == e_s), 1.0, 0.0).astype(BF)
    own = G[0, 0, :, 512:640]
    code_s = dot_plain(own, pick_code)
    w_s = dot_plain(own, pick_w)
    s32 = lax.broadcasted_iota(jnp.int32, (32, 512), 1)
    chosen = code_s == (s32 % 16 + 1).astype(F32)
    weights = jnp.where(chosen, w_s, 0.0)
    w_hi = weights.astype(BF)
    w_lo = (weights - w_hi.astype(F32)).astype(BF)
    e32 = expert_of(s32)
    by_k = jnp.concatenate(
        [jnp.where(chosen & (e32 == ids[:, k : k + 1]), 1.0, 0.0) for k in range(8)], axis=0
    ).astype(BF)
    for copy in back.values():
        copy.wait_recv()
    back_eo = RR[:, :, :, 0:256].reshape(512, 256)
    back_bo = RR[:, :, :, 256:512].reshape(512, 256)
    back_rg = RR[:, :, :, 512:640].reshape(512, 128)
    lo_out[...] = (dot_plain(w_hi, back_eo) + dot_plain(w_lo, back_eo)).astype(BF)
    tg_out[...] = dot_plain(jnp.where(chosen, 1.0, 0.0).astype(BF), back_bo).astype(BF)
    both = dot_plain(by_k, back_rg)
    both = both + pltpu.roll(both, 64, 1)
    k_i = lax.broadcasted_iota(jnp.int32, (32, 8), 1)
    grad = jnp.zeros((32, 8), F32)
    for k in range(8):
        grad = grad + jnp.where(k_i == k, both[32 * k : 32 * k + 32, 0:1], 0.0)
    rg_out[...] = grad

    for store in stores:
        store.wait()
    for copy in sent:
        copy.wait_send()


def local(tokens, expert_ids, route_weights, gate_weight, up_weight, down_weight, output_grad):
    vmem = pl.BlockSpec(memory_space=pltpu.VMEM)
    hbm = pl.BlockSpec(memory_space=pl.ANY)
    wshape = jax.ShapeDtypeStruct((1536, 256), BF)
    dma = pltpu.SemaphoreType.DMA
    lo, tg, rg, gg, ug, dg = pl.pallas_call(
        kernel,
        out_shape=(
            jax.ShapeDtypeStruct((32, 256), BF),
            jax.ShapeDtypeStruct((32, 256), BF),
            jax.ShapeDtypeStruct((32, 8), F32),
            wshape,
            wshape,
            wshape,
        ),
        in_specs=[vmem, vmem, vmem, vmem, hbm, hbm, hbm],
        out_specs=[vmem, vmem, vmem, hbm, hbm, hbm],
        scratch_shapes=[
            pltpu.VMEM((3, 1536, 256), BF),
            pltpu.VMEM((2, NZ, 32, 640), BF),
            pltpu.VMEM((NW, 128, 256), BF),
            pltpu.VMEM((NW, 128, 256), BF),
            pltpu.VMEM((NW, 8, 16, 128), F32),
            pltpu.VMEM((NW, 2, 4, 4, 9, 16, 128), BF),
            pltpu.VMEM((NW, 2, 4, 5, 16, 128), BF),
            pltpu.VMEM((NW, 2, 4, 4, 16, 128), BF),
            pltpu.VMEM((NW, 2, 4, 9, 16, 128), BF),
            pltpu.VMEM((NW, 2, 4, 9, 16, 128), BF),
            pltpu.VMEM((NW, 2, 5, 16, 128), BF),
            pltpu.VMEM((NW, 2, 4, 16, 128), BF),
            pltpu.VMEM((NW, 2, 9, 16, 128), BF),
            pltpu.VMEM((NW, 2, 9, 16, 128), BF),
            pltpu.VMEM((NW, 2, 4, 4, 10, 16, 128), BF),
            pltpu.VMEM((3, 512, 1536), BF),
            pltpu.VMEM((NW, 8, 16, 640), BF),
            pltpu.VMEM((2, NZ, 16, 640), BF),
            pltpu.VMEM((3, 1536, 256), BF),
            dma((3,)),
            dma((3,)),
            dma((2, 9)),
            dma((2, 9)),
            dma((NZ,)),
            dma((NZ,)),
            dma((NW, 2, 2, 2, 3)),
            dma((NW, 2, 2, 2, 3)),
            dma((NW, 2, 2, 2, 3)),
            dma((NW, 2, 2, 2, 3)),
            dma((2, NZ)),
            dma((2, NZ)),
        ],
        compiler_params=pltpu.CompilerParams(
            collective_id=0, has_side_effects=True, vmem_limit_bytes=60 * 1024 * 1024
        ),
    )(
        tokens, expert_ids, route_weights, output_grad,
        gate_weight[0], up_weight[0], down_weight[0],
    )
    return lo, tg, rg, gg[None], ug[None], dg[None]


def solution(mesh):
    placed = (
        P("expert", "dp"),
        P("expert", None),
        P("expert", None),
        P("expert", None, "dp"),
        P("expert", None, "dp"),
        P("expert", None, "dp"),
        P("expert", "dp"),
    )
    return jax.shard_map(
        local,
        mesh=mesh,
        in_specs=placed,
        out_specs=(
            P("expert", "dp"),
            P("expert", "dp"),
            P("expert", None),
            P("expert", None, "dp"),
            P("expert", None, "dp"),
            P("expert", None, "dp"),
        ),
        check_vma=False,
    )
```

```python
import jax
import jax.numpy as jnp
from jax import lax
from jax.experimental import pallas as pl
from jax.experimental.pallas import tpu as pltpu
from jax.sharding import PartitionSpec as P

MESH = pl.DeviceIdType.MESH
BF = jnp.bfloat16
F32 = jnp.float32

WAVES = ((0, 15, 1, 14), (2, 13, 3, 12), (4, 11, 5, 10), (6, 9, 7, 8))
NZ = 16
NW = 4
LAG = 1
STAGES = 9


def dot_last(a, b):
    return lax.dot_general(a, b, (((1,), (1,)), ((), ())), preferred_element_type=F32)


def dot_first(a, b):
    return lax.dot_general(a, b, (((0,), (0,)), ((), ())), preferred_element_type=F32)


def dot_plain(a, b):
    return lax.dot_general(a, b, (((1,), (0,)), ((), ())), preferred_element_type=F32)


def kernel(
    tok, ids, rw, og, wg, wu, wd,
    lo_out, tg_out, rg_out, grads_out,
    W, G, X, GD, WC, S, M1P, M1M, RP, RM, Q1P, Q1M, QP, QM, A, H3, RET, RR, OUT,
    w_sem, o_sem, n_snd, n_rcv, z_snd, z_rcv, b_snd, b_rcv, s_snd, s_rcv, a_snd, a_rcv, t_snd, t_rcv,
):
    dp = lax.axis_index("dp")
    e = lax.axis_index("expert")
    x, y = dp // 4, dp % 4
    z, c = e // 2, e % 2
    pos = (x, y)

    def along(axis, step):
        if axis == 0:
            return {"dp": lax.rem(x + step, 4) * 4 + y}
        return {"dp": x * 4 + lax.rem(y + step, 4)}

    def on_z(step, other):
        return {"expert": lax.rem(z + step, NZ) * 2 + ((1 - c) if other else c)}

    loads = [
        pltpu.make_async_copy(src, W.at[n], w_sem.at[n]) for n, src in enumerate((wg, wu, wd))
    ]
    for load in loads:
        load.start()

    near = [along(axis, step) for axis in (0, 1) for step in (1, 3)]
    near += [on_z(step, False) for step in (1, 2, NZ - 1, NZ - 2)] + [on_z(0, True)]
    barrier = pltpu.get_barrier_semaphore()
    for peer in near:
        pl.semaphore_signal(barrier, inc=1, device_id=peer, device_id_type=MESH)

    sub = lax.broadcasted_iota(jnp.int32, (128, 32), 0)
    ex = sub % 32
    dense = jnp.zeros((128, 32), F32)
    member = jnp.zeros((128, 32), F32)
    ids_f = jnp.zeros((128, 32), F32)
    for k in range(8):
        named = ids[k : k + 1, :]
        hit = ex == named
        dense = dense + jnp.where(hit, rw[k : k + 1, :], 0.0)
        member = member + jnp.where(hit, 1.0, 0.0)
        ids_f = ids_f + jnp.where(sub == k, named.astype(F32), 0.0)
    tri = lax.broadcasted_iota(jnp.int32, (32, 32), 0) < lax.broadcasted_iota(jnp.int32, (32, 32), 1)
    before = dot_plain(member.astype(BF), jnp.where(tri, 1.0, 0.0).astype(BF))
    code = member * (before + 1.0)
    hi = dense.astype(BF)
    rest = dense - hi.astype(F32)
    mid = rest.astype(BF)
    low = (rest - mid.astype(F32)).astype(BF)
    meta = jnp.where(
        sub < 32,
        code,
        jnp.where(sub < 64, hi.astype(F32), jnp.where(sub < 96, mid.astype(F32), low.astype(F32))),
    )
    eye = lax.broadcasted_iota(jnp.int32, (128, 128), 0) == lax.broadcasted_iota(
        jnp.int32, (128, 128), 1
    )
    eye = jnp.where(eye, 1.0, 0.0).astype(BF)
    G[0, 0, :, 0:256] = tok[...]
    G[0, 0, :, 256:512] = og[...]
    G[0, 0, :, 512:640] = dot_first(meta.astype(BF), eye).astype(BF)
    ids_c = dot_first(ids_f.astype(BF), eye)

    pl.semaphore_wait(barrier, len(near))

    sent = []

    def send(src, dst, snd, rcv, to):
        copy = pltpu.make_async_remote_copy(
            src_ref=src, dst_ref=dst, send_sem=snd, recv_sem=rcv, device_id=to, device_id_type=MESH
        )
        copy.start()
        sent.append(copy)
        return copy

    first = []
    for n, step in enumerate((1, NZ - 1, 2, NZ - 2)):
        first.append(
            send(G.at[0, 0], G.at[0, NZ - step], n_snd.at[n], n_rcv.at[n], on_z(step, False))
        )
    sib = {}

    def sib_send(key, at, count):
        n = len(sib)
        sib[key] = send(
            G.at[0, pl.ds(at, count)], G.at[1, pl.ds(at, count)], b_snd.at[n], b_rcv.at[n], on_z(0, True)
        )

    sib_send((0, 0), 0, 1)
    ring = {}
    pumped = [0]

    def pump(upto):
        while pumped[0] < min(upto, 4):
            pumped[0] += 1
            s = pumped[0]
            up, down = (NZ - 2 * s, 2), (2 * s - 1, 1 if s == 4 else 2)
            arrivals = first if s == 1 else [ring[0, s], ring[1, s]]
            for copy in arrivals:
                copy.wait_recv()
            if s < 4:
                n_down = 1 if s == 3 else 2
                ring[0, s + 1] = send(
                    G.at[0, pl.ds(up[0], 2)], G.at[0, pl.ds(up[0] - 2, 2)],
                    z_snd.at[0, s], z_rcv.at[0, s], on_z(2, False),
                )
                ring[1, s + 1] = send(
                    G.at[0, pl.ds(down[0], n_down)], G.at[0, pl.ds(down[0] + 2, n_down)],
                    z_snd.at[1, s], z_rcv.at[1, s], on_z(NZ - 2, False),
                )
            sib_send((s, 0), *up)
            sib_send((s, 1), *down)

    got = set()

    def need(step):
        pump(step)
        for key in sorted(sib):
            if key[0] <= step and key not in got:
                got.add(key)
                sib[key].wait_recv()

    made = {}

    def ring_pair(key, fwd, back, axis):
        for n, (src, dst) in enumerate(fwd):
            made[key, 0, n] = send(src, dst, *sems(key, 0, n), along(axis, 1))
        for n, (src, dst) in enumerate(back):
            made[key, 1, n] = send(src, dst, *sems(key, 1, n), along(axis, 3))

    def sems(key, d, n):
        kind, w, h, ph = key
        if kind == "s":
            return s_snd.at[w, h, ph, d, n], s_rcv.at[w, h, ph, d, n]
        return a_snd.at[w, h, ph, d, n], a_rcv.at[w, h, ph, d, n]

    def arrived(key, d, n):
        made[key, d, n].wait_recv()

    def reduce_start(w, h, ph):
        axis = h if ph == 0 else 1 - h
        i = pos[axis]
        if ph == 0:
            part = lambda t, us: S.at[w, h, t, :, us]
            m1p, m1m, rp, rm = M1P.at[w, h], M1M.at[w, h], RP, RM
            into = lambda r, us: r.at[w, h, :, us]
        else:
            own = pos[h]
            part = lambda t, us: S.at[w, h, own, t, us]
            m1p, m1m, rp, rm = Q1P.at[w, h], Q1M.at[w, h], QP, QM
            into = lambda r, us: r.at[w, h, us]
        L, R = pl.ds(0, 5), pl.ds(5, 4)
        two, nxt, prv = lax.rem(i + 2, 4), lax.rem(i + 1, 4), lax.rem(i + 3, 4)
        ring_pair(
            ("s", w, h, ph),
            ((part(two, L), m1p), (part(nxt, R), into(rp, R))),
            ((part(two, R), m1m), (part(prv, L), into(rm, L))),
            axis,
        )

    def reduce_merge(w, h, ph):
        axis = h if ph == 0 else 1 - h
        i = pos[axis]
        key = ("s", w, h, ph)
        nxt, prv = lax.rem(i + 1, 4), lax.rem(i + 3, 4)
        L, R = pl.ds(0, 5), pl.ds(5, 4)
        if ph == 0:
            part = lambda t, us: S.at[w, h, t, :, us]
            m1p, m1m, rp, rm = M1P.at[w, h], M1M.at[w, h], RP, RM
            into = lambda r, us: r.at[w, h, :, us]
        else:
            own = pos[h]
            part = lambda t, us: S.at[w, h, own, t, us]
            m1p, m1m, rp, rm = Q1P.at[w, h], Q1M.at[w, h], QP, QM
            into = lambda r, us: r.at[w, h, us]
        for d, tgt, us, m1, r in ((0, nxt, L, m1p, rp), (1, prv, R, m1m, rm)):
            arrived(key, d, 0)
            ref = part(tgt, us)
            ref[...] = (ref[...].astype(F32) + m1[...].astype(F32)).astype(BF)
            made[key, d, 2] = send(ref, into(r, us), *sems(key, d, 2), along(axis, 1 if d == 0 else 3))

    def reduce_end(w, h, ph):
        key = ("s", w, h, ph)
        for d in (0, 1):
            arrived(key, d, 1)
            arrived(key, d, 2)
        if ph == 0:
            i = pos[h]
            total = S[w, h, i].astype(F32) + RP[w, h].astype(F32) + RM[w, h].astype(F32)
            S[w, h, i] = total.astype(BF)
            return None
        return S[w, h, pos[h], pos[1 - h]].astype(F32) + QP[w, h].astype(F32) + QM[w, h].astype(F32)

    def gather_start(w, h, ph):
        axis = 1 - h if ph == 0 else h
        i, j = pos[h], pos[1 - h]
        L, R = pl.ds(0, 5), pl.ds(5, 5 - h)
        part = (lambda us: A.at[w, h, i, j, us]) if ph == 0 else (lambda us: A.at[w, h, i, :, us])
        ring_pair(
            ("a", w, h, ph),
            ((part(L), part(L)), (part(R), part(R))),
            ((part(R), part(R)), (part(L), part(L))),
            axis,
        )

    def gather_forward(w, h, ph):
        axis = 1 - h if ph == 0 else h
        key = ("a", w, h, ph)
        i, j = pos[h], pos[1 - h]
        nxt, prv = lax.rem(pos[axis] + 1, 4), lax.rem(pos[axis] + 3, 4)
        L, R = pl.ds(0, 5), pl.ds(5, 5 - h)
        for d, src, us in ((0, prv, L), (1, nxt, R)):
            arrived(key, d, 0)
            ref = A.at[w, h, i, src, us] if ph == 0 else A.at[w, h, src, :, us]
            made[key, d, 2] = send(ref, ref, *sems(key, d, 2), along(axis, 1 if d == 0 else 3))

    def gather_end(w, h, ph):
        for d in (0, 1):
            arrived(("a", w, h, ph), d, 1)
            arrived(("a", w, h, ph), d, 2)

    def partials(w):
        blocks = [(r, o) for r in WAVES[w] for o in (0, 1)]
        need(max((min(r, NZ - r) + 1) // 2 for r in WAVES[w]))
        tokens = jnp.concatenate([G[o, r, :, 0:256] for r, o in blocks], axis=0)
        grads = jnp.concatenate([G[o, r, :, 256:512] for r, o in blocks], axis=0)
        info_in = jnp.concatenate([G[o, r, :, 512:640] for r, o in blocks], axis=0)
        row = lax.broadcasted_iota(jnp.int32, (16, 128), 0)
        col = lax.broadcasted_iota(jnp.int32, (16, 128), 1)
        pick = jnp.where((col == row * 32 + e) & (row < 4), 1.0, 0.0).astype(BF)
        info = dot_last(pick, info_in)
        w_row = info[1:2] + info[2:3] + info[3:4]
        s_i = lax.broadcasted_iota(jnp.int32, (128, 256), 0)
        t_i = lax.broadcasted_iota(jnp.int32, (128, 256), 1)
        sel = (s_i // 16 == t_i // 32) & (info[0:1] == (s_i % 16 + 1).astype(F32))
        sel_b = jnp.where(sel, 1.0, 0.0).astype(BF)
        w_col = jnp.sum(jnp.where(sel, w_row, 0.0), axis=1, keepdims=True)
        rows = dot_plain(sel_b, tokens).astype(BF)
        rows_g = (dot_plain(sel_b, grads) * w_col).astype(BF)
        X[w] = rows
        GD[w] = rows_g
        WC[w] = jnp.broadcast_to(w_col, (128, 128)).reshape(8, 16, 128)
        for t in range(3):
            if w == 0:
                loads[t].wait()
            src = rows if t < 2 else rows_g
            for n in range(6):
                out = dot_last(src, W[t, n * 256 : (n + 1) * 256, :]).astype(BF)
                q = n // 3
                for part in (0, 1):
                    k = (n % 3) * 2 + part
                    h, u = k // 3, (k % 3) * 3 + t
                    for j in range(8):
                        tile = out[16 * j : 16 * j + 16, part * 128 : part * 128 + 128]
                        if h == 0:
                            S[w, 0, j // 2, 2 * (j % 2) + q, u] = tile
                        else:
                            S[w, 1, 2 * (j % 2) + q, j // 2, u] = tile
        for h in (0, 1):
            reduce_start(w, h, 0)

    def nonlinear(w):
        rg = jnp.zeros((16, 1), F32)
        for h in (0, 1):
            total = reduce_end(w, h, 1)
            i, j = pos[h], pos[1 - h]
            for k in range(3):
                gate, up, hid = total[3 * k], total[3 * k + 1], total[3 * k + 2]
                sig = jax.nn.sigmoid(gate)
                silu = gate * sig
                act = (silu * up).astype(BF)
                A[w, h, i, j, 3 * k] = act
                A[w, h, i, j, 3 * k + 1] = (hid * up * (sig * (1.0 + gate * (1.0 - sig)))).astype(BF)
                A[w, h, i, j, 3 * k + 2] = (hid * silu).astype(BF)
                rg = rg + jnp.sum(act.astype(F32) * hid, axis=1, keepdims=True)
        wc = WC[w, 2 * x + y // 2]
        used = wc > 0.0
        rg = jnp.where(used, rg / jnp.where(used, wc, 1.0), 0.0)
        A[w, 0, x, y, 9] = in_two(rg)
        for h in (0, 1):
            gather_start(w, h, 0)

    lane16 = lax.broadcasted_iota(jnp.int32, (16, 128), 1)

    def in_two(v):
        top = v.astype(BF).astype(F32)
        return jnp.where(lane16 < 64, top, v - top).astype(BF)

    back = {}

    def results(w):
        for h in (0, 1):
            gather_end(w, h, 1)
        base = w * 128
        for j in range(8):
            for q in (0, 1):
                for h in (0, 1):
                    for k in range(3):
                        for t in range(3):
                            if h == 0:
                                tile = A[w, 0, j // 2, 2 * (j % 2) + q, 3 * k + t]
                            else:
                                tile = A[w, 1, 2 * (j % 2) + q, j // 2, 3 * k + t]
                            at = q * 768 + (h * 3 + k) * 128
                            H3[t, base + 16 * j : base + 16 * j + 16, at : at + 128] = tile
        eo = dot_plain(H3[0, base : base + 128, :], W[2]).astype(BF)
        bo = dot_plain(H3[1, base : base + 128, :], W[0])
        bo = (bo + dot_plain(H3[2, base : base + 128, :], W[1])).astype(BF)
        for j in range(8):
            r, o = WAVES[w][j // 2], j % 2
            v = A[w, 0, j // 2, 2 * o, 9].astype(F32) + A[w, 0, j // 2, 2 * o + 1, 9].astype(F32)
            v = in_two(v + pltpu.roll(v, 64, 1))
            local = r == 0 and o == 0
            to = RR.at[0, 0] if local else RET.at[w, j]
            to[:, 0:256] = eo[16 * j : 16 * j + 16]
            to[:, 256:512] = bo[16 * j : 16 * j + 16]
            to[:, 512:640] = v
            if not local:
                m = (NZ - r) % NZ
                back[o, m] = send(
                    RET.at[w, j], RR.at[o, m], t_snd.at[o, m], t_rcv.at[o, m], on_z(r, o == 1)
                )

    def stage(k, w):
        if k == 0:
            partials(w)
        elif k == 4:
            nonlinear(w)
        elif k == 8:
            results(w)
        else:
            for h in (0, 1):
                if k == 1:
                    reduce_merge(w, h, 0)
                elif k == 2:
                    reduce_end(w, h, 0)
                    reduce_start(w, h, 1)
                elif k == 3:
                    reduce_merge(w, h, 1)
                elif k == 5:
                    gather_forward(w, h, 0)
                elif k == 6:
                    gather_end(w, h, 0)
                    gather_start(w, h, 1)
                elif k == 7:
                    gather_forward(w, h, 1)

    for tick in range(STAGES + LAG * (NW - 1)):
        pump(1 + tick)
        for w in range(NW):
            k = tick - LAG * w
            if 0 <= k < STAGES:
                stage(k, w)

    rows_x = X[...].reshape(512, 256)
    rows_g = GD[...].reshape(512, 256)
    stores = []
    for t, (n_h, rhs) in enumerate(((1, rows_x), (2, rows_x), (0, rows_g))):
        for n in range(6):
            cols = H3[n_h, :, n * 256 : (n + 1) * 256]
            OUT[t, n * 256 : (n + 1) * 256, :] = dot_first(cols, rhs).astype(BF)
        store = pltpu.make_async_copy(OUT.at[t], grads_out.at[t], o_sem.at[t])
        store.start()
        stores.append(store)

    s_i = lax.broadcasted_iota(jnp.int32, (128, 512), 1)
    l_i = lax.broadcasted_iota(jnp.int32, (128, 512), 0)

    def expert_of(s):
        blk = s // 16
        core = jnp.where(blk < NZ, c, 1 - c)
        return (z + blk % NZ) % NZ * 2 + core

    e_s = expert_of(s_i)
    pick_code = jnp.where(l_i == e_s, 1.0, 0.0).astype(BF)
    pick_w = jnp.where((l_i >= 32) & (l_i % 32 == e_s), 1.0, 0.0).astype(BF)
    own = G[0, 0, :, 512:640]
    code_s = dot_plain(own, pick_code)
    w_s = dot_plain(own, pick_w)
    s32 = lax.broadcasted_iota(jnp.int32, (32, 512), 1)
    chosen = code_s == (s32 % 16 + 1).astype(F32)
    weights = jnp.where(chosen, w_s, 0.0)
    w_hi = weights.astype(BF)
    w_lo = (weights - w_hi.astype(F32)).astype(BF)
    e32 = expert_of(s32)
    by_k = jnp.concatenate(
        [jnp.where(chosen & (e32.astype(F32) == ids_c[:, k : k + 1]), 1.0, 0.0) for k in range(8)], axis=0
    ).astype(BF)
    for copy in back.values():
        copy.wait_recv()
    back_eo = RR[:, :, :, 0:256].reshape(512, 256)
    back_bo = RR[:, :, :, 256:512].reshape(512, 256)
    back_rg = RR[:, :, :, 512:640].reshape(512, 128)
    lo_out[...] = (dot_plain(w_hi, back_eo) + dot_plain(w_lo, back_eo)).astype(BF)
    tg_out[...] = dot_plain(jnp.where(chosen, 1.0, 0.0).astype(BF), back_bo).astype(BF)
    row = lax.broadcasted_iota(jnp.int32, (16, 128), 0)
    col = lax.broadcasted_iota(jnp.int32, (16, 128), 1)
    halves = jnp.where((col == row * 64) & (row < 2), 1.0, 0.0).astype(BF)
    both = dot_last(dot_last(halves, back_rg).astype(BF), by_k)
    both = both[0:1] + both[1:2]
    for k in range(8):
        rg_out[k : k + 1, :] = both[:, 32 * k : 32 * k + 32]

    for store in stores:
        store.wait()
    for copy in sent:
        copy.wait_send()


def copy_out(lo, tg, rg, grads, lo_out, tg_out, rg_out, gg, ug, dg, LO, TG, RG, B, i_sem, o_sem):
    pairs = [(lo, LO, lo_out), (tg, TG, tg_out), (rg, RG, rg_out)]
    for t, dst in enumerate((gg, ug, dg)):
        for n in (0, 1):
            at = pl.ds(768 * n, 768)
            pairs.append((grads.at[t, at], B.at[t, at], dst.at[at]))
    ins = [pltpu.make_async_copy(a, b, i_sem.at[n]) for n, (a, b, _) in enumerate(pairs)]
    outs = [pltpu.make_async_copy(b, c, o_sem.at[n]) for n, (_, b, c) in enumerate(pairs)]
    for copy in ins:
        copy.start()
    for n in range(len(pairs)):
        ins[n].wait()
        outs[n].start()
    for copy in outs:
        copy.wait()


def local(tokens, expert_ids, route_weights, gate_weight, up_weight, down_weight, output_grad):
    vmem = pl.BlockSpec(memory_space=pltpu.VMEM)
    hbm = pl.BlockSpec(memory_space=pl.ANY)
    wshape = jax.ShapeDtypeStruct((1536, 256), BF)
    small = (
        jax.ShapeDtypeStruct((32, 256), BF),
        jax.ShapeDtypeStruct((32, 256), BF),
        jax.ShapeDtypeStruct((8, 32), F32),
    )
    dma = pltpu.SemaphoreType.DMA
    results = pl.pallas_call(
        kernel,
        out_shape=small + (jax.ShapeDtypeStruct((3, 1536, 256), BF),),
        in_specs=[vmem, vmem, vmem, vmem, hbm, hbm, hbm],
        out_specs=[vmem, vmem, vmem, hbm],
        scratch_shapes=[
            pltpu.VMEM((3, 1536, 256), BF),
            pltpu.VMEM((2, NZ, 32, 640), BF),
            pltpu.VMEM((NW, 128, 256), BF),
            pltpu.VMEM((NW, 128, 256), BF),
            pltpu.VMEM((NW, 8, 16, 128), F32),
            pltpu.VMEM((NW, 2, 4, 4, 9, 16, 128), BF),
            pltpu.VMEM((NW, 2, 4, 5, 16, 128), BF),
            pltpu.VMEM((NW, 2, 4, 4, 16, 128), BF),
            pltpu.VMEM((NW, 2, 4, 9, 16, 128), BF),
            pltpu.VMEM((NW, 2, 4, 9, 16, 128), BF),
            pltpu.VMEM((NW, 2, 5, 16, 128), BF),
            pltpu.VMEM((NW, 2, 4, 16, 128), BF),
            pltpu.VMEM((NW, 2, 9, 16, 128), BF),
            pltpu.VMEM((NW, 2, 9, 16, 128), BF),
            pltpu.VMEM((NW, 2, 4, 4, 10, 16, 128), BF),
            pltpu.VMEM((3, 512, 1536), BF),
            pltpu.VMEM((NW, 8, 16, 640), BF),
            pltpu.VMEM((2, NZ, 16, 640), BF),
            pltpu.VMEM((3, 1536, 256), BF),
            dma((3,)),
            dma((3,)),
            dma((4,)),
            dma((4,)),
            dma((2, 4)),
            dma((2, 4)),
            dma((9,)),
            dma((9,)),
            dma((NW, 2, 2, 2, 3)),
            dma((NW, 2, 2, 2, 3)),
            dma((NW, 2, 2, 2, 3)),
            dma((NW, 2, 2, 2, 3)),
            dma((2, NZ)),
            dma((2, NZ)),
        ],
        compiler_params=pltpu.CompilerParams(
            collective_id=0, has_side_effects=True, vmem_limit_bytes=60 * 1024 * 1024
        ),
        name="experts",
    )(
        tokens, expert_ids.T, route_weights.T, output_grad,
        gate_weight[0], up_weight[0], down_weight[0],
    )
    lo, tg, rg, gg, ug, dg = pl.pallas_call(
        copy_out,
        out_shape=small + (wshape, wshape, wshape),
        in_specs=[hbm] * 4,
        out_specs=[hbm] * 6,
        scratch_shapes=[
            pltpu.VMEM((32, 256), BF),
            pltpu.VMEM((32, 256), BF),
            pltpu.VMEM((8, 32), F32),
            pltpu.VMEM((3, 1536, 256), BF),
            dma((9,)),
            dma((9,)),
        ],
        name="copy_out",
    )(*results)
    return lo, tg, rg.T, gg[None], ug[None], dg[None]


def solution(mesh):
    placed = (
        P("expert", "dp"),
        P("expert", None),
        P("expert", None),
        P("expert", None, "dp"),
        P("expert", None, "dp"),
        P("expert", None, "dp"),
        P("expert", "dp"),
    )
    return jax.shard_map(
        local,
        mesh=mesh,
        in_specs=placed,
        out_specs=(
            P("expert", "dp"),
            P("expert", "dp"),
            P("expert", None),
            P("expert", None, "dp"),
            P("expert", None, "dp"),
            P("expert", None, "dp"),
        ),
        check_vma=False,
    )
```

```python
import jax
import jax.numpy as jnp
from jax import lax
from jax.experimental import pallas as pl
from jax.experimental.pallas import tpu as pltpu
from jax.sharding import PartitionSpec as P

MESH = pl.DeviceIdType.MESH
BF = jnp.bfloat16
F32 = jnp.float32

WAVES = ((0, 15, 1, 14), (4, 11, 5, 10), (2, 13, 3, 12), (6, 9, 7, 8))
NZ = 16
NW = 4
ORDER = (
    (0, 0), (1,), (2,), (1, 0, 1), (1, 0, 0), (0, 2), (2, 0, 1), (0, 1), (1, 2, 0), (1, 2, 1), (3,), (4,),
    (1, 1, 1), (1, 1, 0), (0, 3), (2, 1, 0), (2, 2, 0), (2, 1, 1), (1, 3, 1), (1, 3, 0), (3, 1, 1), (2, 2, 1),
    (3, 1, 0), (3, 2, 0), (2, 3, 1), (2, 3, 0), (2, 0, 0), (4, 1), (3, 2, 1), (3, 3, 1), (3, 3, 0), (5, 1, 1),
    (3, 0, 1), (5, 1, 0), (4, 2), (3, 0, 0), (4, 3), (6, 1, 1), (6, 1, 0), (5, 3, 0), (5, 3, 1), (7, 1, 0),
    (5, 2, 1), (7, 1, 1), (6, 3, 0), (6, 3, 1), (5, 2, 0), (4, 0), (8, 1), (7, 3, 0), (7, 3, 1), (5, 0, 0),
    (6, 2, 1), (6, 2, 0), (5, 0, 1), (8, 3), (7, 2, 1), (6, 0, 1), (7, 2, 0), (6, 0, 0), (8, 2), (7, 0, 0),
    (7, 0, 1), (8, 0),
)


def dot_last(a, b):
    return lax.dot_general(a, b, (((1,), (1,)), ((), ())), preferred_element_type=F32)


def dot_first(a, b):
    return lax.dot_general(a, b, (((0,), (0,)), ((), ())), preferred_element_type=F32)


def dot_plain(a, b):
    return lax.dot_general(a, b, (((1,), (0,)), ((), ())), preferred_element_type=F32)


def kernel(
    tok, ids, rw, og, wg, wu, wd,
    lo_out, tg_out, rg_out, grads_out,
    W, G, X, GD, WC, S, M1P, M1M, RP, RM, Q1P, Q1M, QP, QM, A, H3, RET, RR, RETG, RRG, OUT,
    w_sem, o_sem, n_snd, n_rcv, z_snd, z_rcv, b_snd, b_rcv, s_snd, s_rcv, a_snd, a_rcv, t_snd, t_rcv, g_snd, g_rcv,
):
    dp = lax.axis_index("dp")
    e = lax.axis_index("expert")
    x, y = dp // 4, dp % 4
    z, c = e // 2, e % 2
    pos = (x, y)

    def along(axis, step):
        if axis == 0:
            return {"dp": lax.rem(x + step, 4) * 4 + y}
        return {"dp": x * 4 + lax.rem(y + step, 4)}

    def on_z(step, other):
        return {"expert": lax.rem(z + step, NZ) * 2 + ((1 - c) if other else c)}

    loads = [
        pltpu.make_async_copy(src, W.at[n], w_sem.at[n]) for n, src in enumerate((wg, wu, wd))
    ]
    for load in loads:
        load.start()

    near = [along(axis, step) for axis in (0, 1) for step in (1, 3)]
    near += [on_z(step, False) for step in (1, 2, NZ - 1, NZ - 2)] + [on_z(0, True)]
    barrier = pltpu.get_barrier_semaphore()
    for peer in near:
        pl.semaphore_signal(barrier, inc=1, device_id=peer, device_id_type=MESH)

    sub = lax.broadcasted_iota(jnp.int32, (128, 32), 0)
    ex = sub % 32
    dense = jnp.zeros((128, 32), F32)
    member = jnp.zeros((128, 32), F32)
    ids_f = jnp.zeros((128, 32), F32)
    for k in range(8):
        named = ids[k : k + 1, :]
        hit = ex == named
        dense = dense + jnp.where(hit, rw[k : k + 1, :], 0.0)
        member = member + jnp.where(hit, 1.0, 0.0)
        ids_f = ids_f + jnp.where(sub == k, named.astype(F32), 0.0)
    tri = lax.broadcasted_iota(jnp.int32, (32, 32), 0) < lax.broadcasted_iota(jnp.int32, (32, 32), 1)
    before = dot_plain(member.astype(BF), jnp.where(tri, 1.0, 0.0).astype(BF))
    code = member * (before + 1.0)
    hi = dense.astype(BF)
    rest = dense - hi.astype(F32)
    mid = rest.astype(BF)
    low = (rest - mid.astype(F32)).astype(BF)
    meta = jnp.where(
        sub < 32,
        code,
        jnp.where(sub < 64, hi.astype(F32), jnp.where(sub < 96, mid.astype(F32), low.astype(F32))),
    )
    eye = lax.broadcasted_iota(jnp.int32, (128, 128), 0) == lax.broadcasted_iota(
        jnp.int32, (128, 128), 1
    )
    eye = jnp.where(eye, 1.0, 0.0).astype(BF)
    G[0, 0, :, 0:256] = tok[...]
    G[0, 0, :, 256:512] = og[...]
    G[0, 0, :, 512:640] = dot_first(meta.astype(BF), eye).astype(BF)
    ids_c = dot_first(ids_f.astype(BF), eye)

    pl.semaphore_wait(barrier, len(near))

    sent = []

    def send(src, dst, snd, rcv, to):
        copy = pltpu.make_async_remote_copy(
            src_ref=src, dst_ref=dst, send_sem=snd, recv_sem=rcv, device_id=to, device_id_type=MESH
        )
        copy.start()
        sent.append(copy)
        return copy

    first = []
    for n, step in enumerate((2, NZ - 2, 1, NZ - 1)):
        first.append(
            send(G.at[0, 0], G.at[0, NZ - step], n_snd.at[n], n_rcv.at[n], on_z(step, False))
        )
    sib = {}

    def sib_send(key, at, count):
        n = len(sib)
        sib[key] = send(
            G.at[0, pl.ds(at, count)], G.at[1, pl.ds(at, count)], b_snd.at[n], b_rcv.at[n], on_z(0, True)
        )

    sib_send((0, 0), 0, 1)
    ring = {}
    pumped = [0]

    def pump(upto):
        while pumped[0] < min(upto, 4):
            pumped[0] += 1
            s = pumped[0]
            up, down = (NZ - 2 * s, 2), (2 * s - 1, 1 if s == 4 else 2)
            arrivals = first if s == 1 else [ring[0, s], ring[1, s]]
            for copy in arrivals:
                copy.wait_recv()
            if s < 4:
                n_down = 1 if s == 3 else 2
                ring[0, s + 1] = send(
                    G.at[0, pl.ds(up[0], 2)], G.at[0, pl.ds(up[0] - 2, 2)],
                    z_snd.at[0, s], z_rcv.at[0, s], on_z(2, False),
                )
                ring[1, s + 1] = send(
                    G.at[0, pl.ds(down[0], n_down)], G.at[0, pl.ds(down[0] + 2, n_down)],
                    z_snd.at[1, s], z_rcv.at[1, s], on_z(NZ - 2, False),
                )
            sib_send((s, 0), *up)
            sib_send((s, 1), *down)

    got = set()

    def need(step):
        pump(step)
        for key in sorted(sib):
            if key[0] <= step and key not in got:
                got.add(key)
                sib[key].wait_recv()

    made = {}

    def ring_pair(key, fwd, back, axis):
        for n, (src, dst) in enumerate(fwd):
            made[key, 0, n] = send(src, dst, *sems(key, 0, n), along(axis, 1))
        for n, (src, dst) in enumerate(back):
            made[key, 1, n] = send(src, dst, *sems(key, 1, n), along(axis, 3))

    def sems(key, d, n):
        kind, w, h, ph = key
        if kind == "s":
            return s_snd.at[w, h, ph, d, n], s_rcv.at[w, h, ph, d, n]
        return a_snd.at[w, h, ph, d, n], a_rcv.at[w, h, ph, d, n]

    def arrived(key, d, n):
        made[key, d, n].wait_recv()

    def reduce_start(w, h, ph):
        axis = h if ph == 0 else 1 - h
        i = pos[axis]
        if ph == 0:
            part = lambda t, us: S.at[w, h, t, :, us]
            m1p, m1m, rp, rm = M1P.at[w, h], M1M.at[w, h], RP, RM
            into = lambda r, us: r.at[w, h, :, us]
        else:
            own = pos[h]
            part = lambda t, us: S.at[w, h, own, t, us]
            m1p, m1m, rp, rm = Q1P.at[w, h], Q1M.at[w, h], QP, QM
            into = lambda r, us: r.at[w, h, us]
        L, R = pl.ds(0, 5), pl.ds(5, 4)
        two, nxt, prv = lax.rem(i + 2, 4), lax.rem(i + 1, 4), lax.rem(i + 3, 4)
        ring_pair(
            ("s", w, h, ph),
            ((part(two, L), m1p), (part(nxt, R), into(rp, R))),
            ((part(two, R), m1m), (part(prv, L), into(rm, L))),
            axis,
        )

    def reduce_merge(w, h, ph):
        axis = h if ph == 0 else 1 - h
        i = pos[axis]
        key = ("s", w, h, ph)
        nxt, prv = lax.rem(i + 1, 4), lax.rem(i + 3, 4)
        L, R = pl.ds(0, 5), pl.ds(5, 4)
        if ph == 0:
            part = lambda t, us: S.at[w, h, t, :, us]
            m1p, m1m, rp, rm = M1P.at[w, h], M1M.at[w, h], RP, RM
            into = lambda r, us: r.at[w, h, :, us]
        else:
            own = pos[h]
            part = lambda t, us: S.at[w, h, own, t, us]
            m1p, m1m, rp, rm = Q1P.at[w, h], Q1M.at[w, h], QP, QM
            into = lambda r, us: r.at[w, h, us]
        for d, tgt, us, m1, r in ((0, nxt, L, m1p, rp), (1, prv, R, m1m, rm)):
            arrived(key, d, 0)
            ref = part(tgt, us)
            ref[...] = (ref[...].astype(F32) + m1[...].astype(F32)).astype(BF)
            made[key, d, 2] = send(ref, into(r, us), *sems(key, d, 2), along(axis, 1 if d == 0 else 3))

    def reduce_end(w, h, ph):
        key = ("s", w, h, ph)
        for d in (0, 1):
            arrived(key, d, 1)
            arrived(key, d, 2)
        if ph == 0:
            i = pos[h]
            total = S[w, h, i].astype(F32) + RP[w, h].astype(F32) + RM[w, h].astype(F32)
            S[w, h, i] = total.astype(BF)
            return None
        return S[w, h, pos[h], pos[1 - h]].astype(F32) + QP[w, h].astype(F32) + QM[w, h].astype(F32)

    def gather_start(w, h, ph):
        axis = 1 - h if ph == 0 else h
        i, j = pos[h], pos[1 - h]
        L, R = pl.ds(0, 5), pl.ds(5, 5 - h)
        part = (lambda us: A.at[w, h, i, j, us]) if ph == 0 else (lambda us: A.at[w, h, i, :, us])
        ring_pair(
            ("a", w, h, ph),
            ((part(L), part(L)), (part(R), part(R))),
            ((part(R), part(R)), (part(L), part(L))),
            axis,
        )

    def gather_forward(w, h, ph):
        axis = 1 - h if ph == 0 else h
        key = ("a", w, h, ph)
        i, j = pos[h], pos[1 - h]
        nxt, prv = lax.rem(pos[axis] + 1, 4), lax.rem(pos[axis] + 3, 4)
        L, R = pl.ds(0, 5), pl.ds(5, 5 - h)
        for d, src, us in ((0, prv, L), (1, nxt, R)):
            arrived(key, d, 0)
            ref = A.at[w, h, i, src, us] if ph == 0 else A.at[w, h, src, :, us]
            made[key, d, 2] = send(ref, ref, *sems(key, d, 2), along(axis, 1 if d == 0 else 3))

    def gather_end(w, h, ph):
        for d in (0, 1):
            arrived(("a", w, h, ph), d, 1)
            arrived(("a", w, h, ph), d, 2)

    def partials(w):
        blocks = [(r, o) for r in WAVES[w] for o in (0, 1)]
        need(max((min(r, NZ - r) + 1) // 2 for r in WAVES[w]))
        tokens = jnp.concatenate([G[o, r, :, 0:256] for r, o in blocks], axis=0)
        grads = jnp.concatenate([G[o, r, :, 256:512] for r, o in blocks], axis=0)
        info_in = jnp.concatenate([G[o, r, :, 512:640] for r, o in blocks], axis=0)
        row = lax.broadcasted_iota(jnp.int32, (16, 128), 0)
        col = lax.broadcasted_iota(jnp.int32, (16, 128), 1)
        pick = jnp.where((col == row * 32 + e) & (row < 4), 1.0, 0.0).astype(BF)
        info = dot_last(pick, info_in)
        w_row = info[1:2] + info[2:3] + info[3:4]
        s_i = lax.broadcasted_iota(jnp.int32, (128, 256), 0)
        t_i = lax.broadcasted_iota(jnp.int32, (128, 256), 1)
        sel = (s_i // 16 == t_i // 32) & (info[0:1] == (s_i % 16 + 1).astype(F32))
        sel_b = jnp.where(sel, 1.0, 0.0).astype(BF)
        w_col = jnp.sum(jnp.where(sel, w_row, 0.0), axis=1, keepdims=True)
        rows = dot_plain(sel_b, tokens).astype(BF)
        rows_g = (dot_plain(sel_b, grads) * w_col).astype(BF)
        X[w] = rows
        GD[w] = rows_g
        WC[w] = jnp.broadcast_to(w_col, (128, 128)).reshape(8, 16, 128)
        for t in range(3):
            if w == 0:
                loads[t].wait()
            src = rows if t < 2 else rows_g
            for n in range(6):
                out = dot_last(src, W[t, n * 256 : (n + 1) * 256, :]).astype(BF)
                q = n // 3
                for part in (0, 1):
                    k = (n % 3) * 2 + part
                    h, u = k // 3, (k % 3) * 3 + t
                    for j in range(8):
                        tile = out[16 * j : 16 * j + 16, part * 128 : part * 128 + 128]
                        if h == 0:
                            S[w, 0, j // 2, 2 * (j % 2) + q, u] = tile
                        else:
                            S[w, 1, 2 * (j % 2) + q, j // 2, u] = tile
        for h in (0, 1):
            reduce_start(w, h, 0)

    def nonlinear(w):
        rg = jnp.zeros((16, 1), F32)
        for h in (0, 1):
            total = reduce_end(w, h, 1)
            i, j = pos[h], pos[1 - h]
            for k in range(3):
                gate, up, hid = total[3 * k], total[3 * k + 1], total[3 * k + 2]
                sig = jax.nn.sigmoid(gate)
                silu = gate * sig
                act = (silu * up).astype(BF)
                A[w, h, i, j, 3 * k] = act
                A[w, h, i, j, 3 * k + 1] = (hid * up * (sig * (1.0 + gate * (1.0 - sig)))).astype(BF)
                A[w, h, i, j, 3 * k + 2] = (hid * silu).astype(BF)
                rg = rg + jnp.sum(act.astype(F32) * hid, axis=1, keepdims=True)
        wc = WC[w, 2 * x + y // 2]
        used = wc > 0.0
        rg = jnp.where(used, rg / jnp.where(used, wc, 1.0), 0.0)
        A[w, 0, x, y, 9] = in_two(rg)
        for h in (0, 1):
            gather_start(w, h, 0)

    lane16 = lax.broadcasted_iota(jnp.int32, (16, 128), 1)
    row16 = lax.broadcasted_iota(jnp.int32, (16, 128), 0)

    def in_two(v):
        top = v.astype(BF).astype(F32)
        return jnp.where(lane16 < 64, top, v - top).astype(BF)

    back = {}

    def results(w):
        for h in (0, 1):
            gather_end(w, h, 1)
        base = w * 128
        for j in range(8):
            for q in (0, 1):
                for h in (0, 1):
                    for k in range(3):
                        for t in range(3):
                            if h == 0:
                                tile = A[w, 0, j // 2, 2 * (j % 2) + q, 3 * k + t]
                            else:
                                tile = A[w, 1, 2 * (j % 2) + q, j // 2, 3 * k + t]
                            at = q * 768 + (h * 3 + k) * 128
                            H3[t, base + 16 * j : base + 16 * j + 16, at : at + 128] = tile
        eo = dot_plain(H3[0, base : base + 128, :], W[2]).astype(BF)
        bo = dot_plain(H3[1, base : base + 128, :], W[0])
        bo = (bo + dot_plain(H3[2, base : base + 128, :], W[1])).astype(BF)
        for j in range(8):
            r, o = WAVES[w][j // 2], j % 2
            v = A[w, 0, j // 2, 2 * o, 9].astype(F32) + A[w, 0, j // 2, 2 * o + 1, 9].astype(F32)
            v = v + pltpu.roll(v, 64, 1)
            v = jnp.sum(jnp.where(row16 == lane16, v, 0.0), axis=0, keepdims=True)
            local = r == 0 and o == 0
            to = RR.at[0, 0] if local else RET.at[w, j]
            to[:, 0:256] = eo[16 * j : 16 * j + 16]
            to[:, 256:512] = bo[16 * j : 16 * j + 16]
            (RRG.at[0, 0] if local else RETG.at[w, j])[...] = v
            if not local:
                m = (NZ - r) % NZ
                back[o, m] = send(
                    RET.at[w, j], RR.at[o, m], t_snd.at[o, m], t_rcv.at[o, m], on_z(r, o == 1)
                )
                back["g", o, m] = send(
                    RETG.at[w, j], RRG.at[o, m], g_snd.at[o, m], g_rcv.at[o, m], on_z(r, o == 1)
                )

    def stage(k, w, h=0):
        if k == 0:
            partials(w)
        elif k == 1:
            reduce_merge(w, h, 0)
        elif k == 2:
            reduce_end(w, h, 0)
            reduce_start(w, h, 1)
        elif k == 3:
            reduce_merge(w, h, 1)
        elif k == 4:
            nonlinear(w)
        elif k == 5:
            gather_forward(w, h, 0)
        elif k == 6:
            gather_end(w, h, 0)
            gather_start(w, h, 1)
        elif k == 7:
            gather_forward(w, h, 1)
        else:
            results(w)

    for item in ORDER:
        if len(item) == 1:
            pump(item[0])
        else:
            stage(*item)

    rows_x = X[...].reshape(512, 256)
    rows_g = GD[...].reshape(512, 256)
    stores = []
    for t, (n_h, rhs) in enumerate(((1, rows_x), (2, rows_x), (0, rows_g))):
        for n in range(6):
            cols = H3[n_h, :, n * 256 : (n + 1) * 256]
            OUT[t, n * 256 : (n + 1) * 256, :] = dot_first(cols, rhs).astype(BF)
        store = pltpu.make_async_copy(OUT.at[t], grads_out.at[t], o_sem.at[t])
        store.start()
        stores.append(store)

    s_i = lax.broadcasted_iota(jnp.int32, (128, 512), 1)
    l_i = lax.broadcasted_iota(jnp.int32, (128, 512), 0)

    def expert_of(s):
        blk = s // 16
        core = jnp.where(blk < NZ, c, 1 - c)
        return (z + blk % NZ) % NZ * 2 + core

    e_s = expert_of(s_i)
    pick_code = jnp.where(l_i == e_s, 1.0, 0.0).astype(BF)
    pick_w = jnp.where((l_i >= 32) & (l_i % 32 == e_s), 1.0, 0.0).astype(BF)
    own = G[0, 0, :, 512:640]
    code_s = dot_plain(own, pick_code)
    w_s = dot_plain(own, pick_w)
    s32 = lax.broadcasted_iota(jnp.int32, (32, 512), 1)
    chosen = code_s == (s32 % 16 + 1).astype(F32)
    weights = jnp.where(chosen, w_s, 0.0)
    w_hi = weights.astype(BF)
    w_lo = (weights - w_hi.astype(F32)).astype(BF)
    e32 = expert_of(s32)
    by_k = jnp.concatenate(
        [jnp.where(chosen & (e32.astype(F32) == ids_c[:, k : k + 1]), 1.0, 0.0) for k in range(8)], axis=0
    ).astype(BF)
    for copy in back.values():
        copy.wait_recv()
    back_eo = RR[:, :, :, 0:256].reshape(512, 256)
    back_bo = RR[:, :, :, 256:512].reshape(512, 256)
    lo_out[...] = (dot_plain(w_hi, back_eo) + dot_plain(w_lo, back_eo)).astype(BF)
    tg_out[...] = dot_plain(jnp.where(chosen, 1.0, 0.0).astype(BF), back_bo).astype(BF)
    rg_b = RRG[...].reshape(32, 128)
    rg_hi = rg_b.astype(BF)
    rg_lo = (rg_b - rg_hi.astype(F32)).astype(BF)
    spread = jnp.where(l_i == s_i % 16, 1.0, 0.0).astype(BF)
    block = lax.broadcasted_iota(jnp.int32, (32, 512), 0) == s32 // 16
    rows2 = [
        jnp.sum(jnp.where(block, dot_plain(v, spread), 0.0), axis=0, keepdims=True)
        for v in (rg_hi, rg_lo)
    ]
    first_row = lax.broadcasted_iota(jnp.int32, (16, 512), 0) == 0
    both = dot_last(jnp.where(first_row, rows2[0], rows2[1]).astype(BF), by_k)
    both = both[0:1] + both[1:2]
    for k in range(8):
        rg_out[k : k + 1, :] = both[:, 32 * k : 32 * k + 32]

    for store in stores:
        store.wait()
    for copy in sent:
        copy.wait_send()


def copy_out(lo, tg, rg, grads, lo_out, tg_out, rg_out, gg, ug, dg, LO, TG, RG, B, i_sem, o_sem):
    pairs = [(lo, LO, lo_out), (tg, TG, tg_out), (rg, RG, rg_out)]
    for t, dst in enumerate((gg, ug, dg)):
        for n in (0, 1):
            at = pl.ds(768 * n, 768)
            pairs.append((grads.at[t, at], B.at[t, at], dst.at[at]))
    ins = [pltpu.make_async_copy(a, b, i_sem.at[n]) for n, (a, b, _) in enumerate(pairs)]
    outs = [pltpu.make_async_copy(b, c, o_sem.at[n]) for n, (_, b, c) in enumerate(pairs)]
    for copy in ins:
        copy.start()
    for n in range(len(pairs)):
        ins[n].wait()
        outs[n].start()
    for copy in outs:
        copy.wait()


def local(tokens, expert_ids, route_weights, gate_weight, up_weight, down_weight, output_grad):
    vmem = pl.BlockSpec(memory_space=pltpu.VMEM)
    hbm = pl.BlockSpec(memory_space=pl.ANY)
    wshape = jax.ShapeDtypeStruct((1536, 256), BF)
    small = (
        jax.ShapeDtypeStruct((32, 256), BF),
        jax.ShapeDtypeStruct((32, 256), BF),
        jax.ShapeDtypeStruct((8, 32), F32),
    )
    dma = pltpu.SemaphoreType.DMA
    results = pl.pallas_call(
        kernel,
        out_shape=small + (jax.ShapeDtypeStruct((3, 1536, 256), BF),),
        in_specs=[vmem, vmem, vmem, vmem, hbm, hbm, hbm],
        out_specs=[vmem, vmem, vmem, hbm],
        scratch_shapes=[
            pltpu.VMEM((3, 1536, 256), BF),
            pltpu.VMEM((2, NZ, 32, 640), BF),
            pltpu.VMEM((NW, 128, 256), BF),
            pltpu.VMEM((NW, 128, 256), BF),
            pltpu.VMEM((NW, 8, 16, 128), F32),
            pltpu.VMEM((NW, 2, 4, 4, 9, 16, 128), BF),
            pltpu.VMEM((NW, 2, 4, 5, 16, 128), BF),
            pltpu.VMEM((NW, 2, 4, 4, 16, 128), BF),
            pltpu.VMEM((NW, 2, 4, 9, 16, 128), BF),
            pltpu.VMEM((NW, 2, 4, 9, 16, 128), BF),
            pltpu.VMEM((NW, 2, 5, 16, 128), BF),
            pltpu.VMEM((NW, 2, 4, 16, 128), BF),
            pltpu.VMEM((NW, 2, 9, 16, 128), BF),
            pltpu.VMEM((NW, 2, 9, 16, 128), BF),
            pltpu.VMEM((NW, 2, 4, 4, 10, 16, 128), BF),
            pltpu.VMEM((3, 512, 1536), BF),
            pltpu.VMEM((NW, 8, 16, 512), BF),
            pltpu.VMEM((2, NZ, 16, 512), BF),
            pltpu.VMEM((NW, 8, 1, 128), F32),
            pltpu.VMEM((2, NZ, 1, 128), F32),
            pltpu.VMEM((3, 1536, 256), BF),
            dma((3,)),
            dma((3,)),
            dma((4,)),
            dma((4,)),
            dma((2, 4)),
            dma((2, 4)),
            dma((9,)),
            dma((9,)),
            dma((NW, 2, 2, 2, 3)),
            dma((NW, 2, 2, 2, 3)),
            dma((NW, 2, 2, 2, 3)),
            dma((NW, 2, 2, 2, 3)),
            dma((2, NZ)),
            dma((2, NZ)),
            dma((2, NZ)),
            dma((2, NZ)),
        ],
        compiler_params=pltpu.CompilerParams(
            collective_id=0, has_side_effects=True, vmem_limit_bytes=60 * 1024 * 1024
        ),
        name="experts",
    )(
        tokens, expert_ids.T, route_weights.T, output_grad,
        gate_weight[0], up_weight[0], down_weight[0],
    )
    lo, tg, rg, gg, ug, dg = pl.pallas_call(
        copy_out,
        out_shape=small + (wshape, wshape, wshape),
        in_specs=[hbm] * 4,
        out_specs=[hbm] * 6,
        scratch_shapes=[
            pltpu.VMEM((32, 256), BF),
            pltpu.VMEM((32, 256), BF),
            pltpu.VMEM((8, 32), F32),
            pltpu.VMEM((3, 1536, 256), BF),
            dma((9,)),
            dma((9,)),
        ],
        name="copy_out",
    )(*results)
    return lo, tg, rg.T, gg[None], ug[None], dg[None]


def solution(mesh):
    placed = (
        P("expert", "dp"),
        P("expert", None),
        P("expert", None),
        P("expert", None, "dp"),
        P("expert", None, "dp"),
        P("expert", None, "dp"),
        P("expert", "dp"),
    )
    return jax.shard_map(
        local,
        mesh=mesh,
        in_specs=placed,
        out_specs=(
            P("expert", "dp"),
            P("expert", "dp"),
            P("expert", None),
            P("expert", None, "dp"),
            P("expert", None, "dp"),
            P("expert", None, "dp"),
        ),
        check_vma=False,
    )
```

```python
import jax
import jax.numpy as jnp
from jax import lax
from jax.experimental import pallas as pl
from jax.experimental.pallas import tpu as pltpu
from jax.sharding import PartitionSpec as P

MESH = pl.DeviceIdType.MESH
BF = jnp.bfloat16
F32 = jnp.float32

WAVES = ((0, 15, 1, 14), (4, 11, 5, 10), (2, 13, 3, 12), (6, 9, 7, 8))
NZ = 16
NW = 4
ORDER = (
    (1,), (0, 0), (2,), (1, 0, 1), (1, 0, 0), (0, 2), (2, 0, 1), (0, 1), (1, 2, 1), (3, 0, 1), (3,), (4,),
    (1, 2, 0), (1, 1, 1), (1, 1, 0), (0, 3), (2, 1, 0), (2, 1, 1), (2, 2, 1), (2, 2, 0), (1, 3, 1), (1, 3, 0),
    (3, 1, 1), (3, 1, 0), (3, 2, 0), (2, 3, 1), (2, 3, 0), (4, 1, 1), (4, 1, 0), (3, 2, 1), (3, 3, 1),
    (3, 3, 0), (5, 1, 0), (5, 1, 1), (2, 0, 0), (4, 2, 1), (4, 2, 0), (4, 3, 1), (4, 3, 0), (6, 1, 0),
    (6, 1, 1), (5, 3, 1), (3, 0, 0), (5, 3, 0), (7, 1, 0), (7, 1, 1), (5, 2, 0), (4, 0, 1), (5, 2, 1),
    (6, 3, 1), (6, 3, 0), (4, 0, 0), (8, 1), (7, 3, 0), (7, 3, 1), (6, 2, 0), (5, 0, 1), (6, 2, 1), (8, 3),
    (7, 2, 0), (5, 0, 0), (7, 2, 1), (6, 0, 1), (6, 0, 0), (8, 2), (7, 0, 0), (7, 0, 1), (8, 0),
)


def dot_last(a, b):
    return lax.dot_general(a, b, (((1,), (1,)), ((), ())), preferred_element_type=F32)


def dot_first(a, b):
    return lax.dot_general(a, b, (((0,), (0,)), ((), ())), preferred_element_type=F32)


def dot_plain(a, b):
    return lax.dot_general(a, b, (((1,), (0,)), ((), ())), preferred_element_type=F32)


def kernel(
    tok, ids, rw, og, wg, wu, wd,
    lo_out, tg_out, rg_out, grads_out,
    W, G, X, GD, WC, S, M1P, M1M, RP, RM, Q1P, Q1M, QP, QM, A, H3, RET, RR, RETG, RRG, OUT,
    w_sem, o_sem, n_snd, n_rcv, z_snd, z_rcv, b_snd, b_rcv, s_snd, s_rcv, a_snd, a_rcv, t_snd, t_rcv, g_snd, g_rcv,
):
    dp = lax.axis_index("dp")
    e = lax.axis_index("expert")
    x, y = dp // 4, dp % 4
    z, c = e // 2, e % 2
    pos = (x, y)

    def along(axis, step):
        if axis == 0:
            return {"dp": lax.rem(x + step, 4) * 4 + y}
        return {"dp": x * 4 + lax.rem(y + step, 4)}

    def on_z(step, other):
        return {"expert": lax.rem(z + step, NZ) * 2 + ((1 - c) if other else c)}

    loads = [
        pltpu.make_async_copy(src, W.at[n], w_sem.at[n]) for n, src in enumerate((wg, wu, wd))
    ]
    for load in loads:
        load.start()

    near = [along(axis, step) for axis in (0, 1) for step in (1, 3)]
    near += [on_z(step, False) for step in (1, 2, NZ - 1, NZ - 2)] + [on_z(0, True)]
    barrier = pltpu.get_barrier_semaphore()
    for peer in near:
        pl.semaphore_signal(barrier, inc=1, device_id=peer, device_id_type=MESH)

    sub = lax.broadcasted_iota(jnp.int32, (128, 32), 0)
    ex = sub % 32
    dense = jnp.zeros((128, 32), F32)
    member = jnp.zeros((128, 32), F32)
    ids_f = jnp.zeros((128, 32), F32)
    for k in range(8):
        named = ids[k : k + 1, :]
        hit = ex == named
        dense = dense + jnp.where(hit, rw[k : k + 1, :], 0.0)
        member = member + jnp.where(hit, 1.0, 0.0)
        ids_f = ids_f + jnp.where(sub == k, named.astype(F32), 0.0)
    tri = lax.broadcasted_iota(jnp.int32, (32, 32), 0) < lax.broadcasted_iota(jnp.int32, (32, 32), 1)
    before = dot_plain(member.astype(BF), jnp.where(tri, 1.0, 0.0).astype(BF))
    code = member * (before + 1.0)
    hi = dense.astype(BF)
    rest = dense - hi.astype(F32)
    mid = rest.astype(BF)
    low = (rest - mid.astype(F32)).astype(BF)
    meta = jnp.where(
        sub < 32,
        code,
        jnp.where(sub < 64, hi.astype(F32), jnp.where(sub < 96, mid.astype(F32), low.astype(F32))),
    )
    eye = lax.broadcasted_iota(jnp.int32, (128, 128), 0) == lax.broadcasted_iota(
        jnp.int32, (128, 128), 1
    )
    eye = jnp.where(eye, 1.0, 0.0).astype(BF)
    G[0, 0, :, 0:256] = tok[...]
    G[0, 0, :, 256:512] = og[...]
    G[0, 0, :, 512:640] = dot_first(meta.astype(BF), eye).astype(BF)
    ids_c = dot_first(ids_f.astype(BF), eye)

    pl.semaphore_wait(barrier, len(near))

    sent = []

    def send(src, dst, snd, rcv, to):
        copy = pltpu.make_async_remote_copy(
            src_ref=src, dst_ref=dst, send_sem=snd, recv_sem=rcv, device_id=to, device_id_type=MESH
        )
        copy.start()
        sent.append(copy)
        return copy

    first = []
    for n, step in enumerate((2, NZ - 2, 1, NZ - 1)):
        first.append(
            send(G.at[0, 0], G.at[0, NZ - step], n_snd.at[n], n_rcv.at[n], on_z(step, False))
        )
    sib = {}

    def sib_send(key, at, count):
        n = len(sib)
        sib[key] = send(
            G.at[0, pl.ds(at, count)], G.at[1, pl.ds(at, count)], b_snd.at[n], b_rcv.at[n], on_z(0, True)
        )

    sib_send((0, 0), 0, 1)
    ring = {}
    pumped = [0]

    def pump(upto):
        while pumped[0] < min(upto, 4):
            pumped[0] += 1
            s = pumped[0]
            up, down = (NZ - 2 * s, 2), (2 * s - 1, 1 if s == 4 else 2)
            arrivals = first if s == 1 else [ring[0, s], ring[1, s]]
            for copy in arrivals:
                copy.wait_recv()
            if s < 4:
                n_down = 1 if s == 3 else 2
                ring[0, s + 1] = send(
                    G.at[0, pl.ds(up[0], 2)], G.at[0, pl.ds(up[0] - 2, 2)],
                    z_snd.at[0, s], z_rcv.at[0, s], on_z(2, False),
                )
                ring[1, s + 1] = send(
                    G.at[0, pl.ds(down[0], n_down)], G.at[0, pl.ds(down[0] + 2, n_down)],
                    z_snd.at[1, s], z_rcv.at[1, s], on_z(NZ - 2, False),
                )
            sib_send((s, 0), *up)
            sib_send((s, 1), *down)

    got = set()

    def need(step):
        pump(step)
        for key in sorted(sib):
            if key[0] <= step and key not in got:
                got.add(key)
                sib[key].wait_recv()

    made = {}

    def ring_pair(key, fwd, back, axis):
        for n, (src, dst) in enumerate(fwd):
            made[key, 0, n] = send(src, dst, *sems(key, 0, n), along(axis, 1))
        for n, (src, dst) in enumerate(back):
            made[key, 1, n] = send(src, dst, *sems(key, 1, n), along(axis, 3))

    def sems(key, d, n):
        kind, w, h, ph = key
        if kind == "s":
            return s_snd.at[w, h, ph, d, n], s_rcv.at[w, h, ph, d, n]
        return a_snd.at[w, h, ph, d, n], a_rcv.at[w, h, ph, d, n]

    def arrived(key, d, n):
        made[key, d, n].wait_recv()

    def reduce_start(w, h, ph):
        axis = h if ph == 0 else 1 - h
        i = pos[axis]
        if ph == 0:
            part = lambda t, us: S.at[w, h, t, :, us]
            m1p, m1m, rp, rm = M1P.at[w, h], M1M.at[w, h], RP, RM
            into = lambda r, us: r.at[w, h, :, us]
        else:
            own = pos[h]
            part = lambda t, us: S.at[w, h, own, t, us]
            m1p, m1m, rp, rm = Q1P.at[w, h], Q1M.at[w, h], QP, QM
            into = lambda r, us: r.at[w, h, us]
        L, R = pl.ds(0, 5), pl.ds(5, 4)
        two, nxt, prv = lax.rem(i + 2, 4), lax.rem(i + 1, 4), lax.rem(i + 3, 4)
        ring_pair(
            ("s", w, h, ph),
            ((part(two, L), m1p), (part(nxt, R), into(rp, R))),
            ((part(two, R), m1m), (part(prv, L), into(rm, L))),
            axis,
        )

    def reduce_merge(w, h, ph):
        axis = h if ph == 0 else 1 - h
        i = pos[axis]
        key = ("s", w, h, ph)
        nxt, prv = lax.rem(i + 1, 4), lax.rem(i + 3, 4)
        L, R = pl.ds(0, 5), pl.ds(5, 4)
        if ph == 0:
            part = lambda t, us: S.at[w, h, t, :, us]
            m1p, m1m, rp, rm = M1P.at[w, h], M1M.at[w, h], RP, RM
            into = lambda r, us: r.at[w, h, :, us]
        else:
            own = pos[h]
            part = lambda t, us: S.at[w, h, own, t, us]
            m1p, m1m, rp, rm = Q1P.at[w, h], Q1M.at[w, h], QP, QM
            into = lambda r, us: r.at[w, h, us]
        for d, tgt, us, m1, r in ((0, nxt, L, m1p, rp), (1, prv, R, m1m, rm)):
            arrived(key, d, 0)
            ref = part(tgt, us)
            ref[...] = (ref[...].astype(F32) + m1[...].astype(F32)).astype(BF)
            made[key, d, 2] = send(ref, into(r, us), *sems(key, d, 2), along(axis, 1 if d == 0 else 3))

    def reduce_end(w, h, ph):
        key = ("s", w, h, ph)
        for d in (0, 1):
            arrived(key, d, 1)
            arrived(key, d, 2)
        if ph == 0:
            i = pos[h]
            total = S[w, h, i].astype(F32) + RP[w, h].astype(F32) + RM[w, h].astype(F32)
            S[w, h, i] = total.astype(BF)
            return None
        return S[w, h, pos[h], pos[1 - h]].astype(F32) + QP[w, h].astype(F32) + QM[w, h].astype(F32)

    def gather_start(w, h, ph):
        axis = 1 - h if ph == 0 else h
        i, j = pos[h], pos[1 - h]
        L, R = pl.ds(0, 5), pl.ds(5, 5 - h)
        part = (lambda us: A.at[w, h, i, j, us]) if ph == 0 else (lambda us: A.at[w, h, i, :, us])
        ring_pair(
            ("a", w, h, ph),
            ((part(L), part(L)), (part(R), part(R))),
            ((part(R), part(R)), (part(L), part(L))),
            axis,
        )

    def gather_forward(w, h, ph):
        axis = 1 - h if ph == 0 else h
        key = ("a", w, h, ph)
        i, j = pos[h], pos[1 - h]
        nxt, prv = lax.rem(pos[axis] + 1, 4), lax.rem(pos[axis] + 3, 4)
        L, R = pl.ds(0, 5), pl.ds(5, 5 - h)
        for d, src, us in ((0, prv, L), (1, nxt, R)):
            arrived(key, d, 0)
            ref = A.at[w, h, i, src, us] if ph == 0 else A.at[w, h, src, :, us]
            made[key, d, 2] = send(ref, ref, *sems(key, d, 2), along(axis, 1 if d == 0 else 3))

    def gather_end(w, h, ph):
        for d in (0, 1):
            arrived(("a", w, h, ph), d, 1)
            arrived(("a", w, h, ph), d, 2)

    def partials(w):
        blocks = [(r, o) for r in WAVES[w] for o in (0, 1)]
        need(max((min(r, NZ - r) + 1) // 2 for r in WAVES[w]))
        tokens = jnp.concatenate([G[o, r, :, 0:256] for r, o in blocks], axis=0)
        grads = jnp.concatenate([G[o, r, :, 256:512] for r, o in blocks], axis=0)
        info_in = jnp.concatenate([G[o, r, :, 512:640] for r, o in blocks], axis=0)
        row = lax.broadcasted_iota(jnp.int32, (16, 128), 0)
        col = lax.broadcasted_iota(jnp.int32, (16, 128), 1)
        pick = jnp.where((col == row * 32 + e) & (row < 4), 1.0, 0.0).astype(BF)
        info = dot_last(pick, info_in)
        w_row = info[1:2] + info[2:3] + info[3:4]
        s_i = lax.broadcasted_iota(jnp.int32, (128, 256), 0)
        t_i = lax.broadcasted_iota(jnp.int32, (128, 256), 1)
        sel = (s_i // 16 == t_i // 32) & (info[0:1] == (s_i % 16 + 1).astype(F32))
        sel_b = jnp.where(sel, 1.0, 0.0).astype(BF)
        w_col = jnp.sum(jnp.where(sel, w_row, 0.0), axis=1, keepdims=True)
        rows = dot_plain(sel_b, tokens).astype(BF)
        rows_g = (dot_plain(sel_b, grads) * w_col).astype(BF)
        X[w] = rows
        GD[w] = rows_g
        WC[w] = jnp.broadcast_to(w_col, (128, 128)).reshape(8, 16, 128)
        for t in range(3):
            if w == 0:
                loads[t].wait()
            src = rows if t < 2 else rows_g
            for n in range(6):
                out = dot_last(src, W[t, n * 256 : (n + 1) * 256, :]).astype(BF)
                q = n // 3
                for part in (0, 1):
                    k = (n % 3) * 2 + part
                    h, u = k // 3, (k % 3) * 3 + t
                    for j in range(8):
                        tile = out[16 * j : 16 * j + 16, part * 128 : part * 128 + 128]
                        if h == 0:
                            S[w, 0, j // 2, 2 * (j % 2) + q, u] = tile
                        else:
                            S[w, 1, 2 * (j % 2) + q, j // 2, u] = tile
        for h in (0, 1):
            reduce_start(w, h, 0)

    route = {}

    def nonlinear(w, h):
        rg = route.get(w, jnp.zeros((16, 1), F32))
        total = reduce_end(w, h, 1)
        i, j = pos[h], pos[1 - h]
        for k in range(3):
            gate, up, hid = total[3 * k], total[3 * k + 1], total[3 * k + 2]
            sig = jax.nn.sigmoid(gate)
            silu = gate * sig
            act = (silu * up).astype(BF)
            A[w, h, i, j, 3 * k] = act
            A[w, h, i, j, 3 * k + 1] = (hid * up * (sig * (1.0 + gate * (1.0 - sig)))).astype(BF)
            A[w, h, i, j, 3 * k + 2] = (hid * silu).astype(BF)
            rg = rg + jnp.sum(act.astype(F32) * hid, axis=1, keepdims=True)
        route[w] = rg
        if h == 0:
            wc = WC[w, 2 * x + y // 2]
            used = wc > 0.0
            rg = jnp.where(used, rg / jnp.where(used, wc, 1.0), 0.0)
            A[w, 0, x, y, 9] = in_two(rg)
        gather_start(w, h, 0)

    lane16 = lax.broadcasted_iota(jnp.int32, (16, 128), 1)
    row16 = lax.broadcasted_iota(jnp.int32, (16, 128), 0)

    def in_two(v):
        top = v.astype(BF).astype(F32)
        return jnp.where(lane16 < 64, top, v - top).astype(BF)

    back = {}

    def results(w):
        for h in (0, 1):
            gather_end(w, h, 1)
        base = w * 128
        for j in range(8):
            for q in (0, 1):
                for h in (0, 1):
                    for k in range(3):
                        for t in range(3):
                            if h == 0:
                                tile = A[w, 0, j // 2, 2 * (j % 2) + q, 3 * k + t]
                            else:
                                tile = A[w, 1, 2 * (j % 2) + q, j // 2, 3 * k + t]
                            at = q * 768 + (h * 3 + k) * 128
                            H3[t, base + 16 * j : base + 16 * j + 16, at : at + 128] = tile
        eo = dot_plain(H3[0, base : base + 128, :], W[2]).astype(BF)
        bo = dot_plain(H3[1, base : base + 128, :], W[0])
        bo = (bo + dot_plain(H3[2, base : base + 128, :], W[1])).astype(BF)
        for j in range(8):
            r, o = WAVES[w][j // 2], j % 2
            v = A[w, 0, j // 2, 2 * o, 9].astype(F32) + A[w, 0, j // 2, 2 * o + 1, 9].astype(F32)
            v = v + pltpu.roll(v, 64, 1)
            v = jnp.sum(jnp.where(row16 == lane16, v, 0.0), axis=0, keepdims=True)
            local = r == 0 and o == 0
            to = RR.at[0, 0] if local else RET.at[w, j]
            to[:, 0:256] = eo[16 * j : 16 * j + 16]
            to[:, 256:512] = bo[16 * j : 16 * j + 16]
            (RRG.at[0, 0] if local else RETG.at[w, j])[...] = v
            if not local:
                m = (NZ - r) % NZ
                back[o, m] = send(
                    RET.at[w, j], RR.at[o, m], t_snd.at[o, m], t_rcv.at[o, m], on_z(r, o == 1)
                )
                back["g", o, m] = send(
                    RETG.at[w, j], RRG.at[o, m], g_snd.at[o, m], g_rcv.at[o, m], on_z(r, o == 1)
                )

    def stage(k, w, h=0):
        if k == 0:
            partials(w)
        elif k == 1:
            reduce_merge(w, h, 0)
        elif k == 2:
            reduce_end(w, h, 0)
            reduce_start(w, h, 1)
        elif k == 3:
            reduce_merge(w, h, 1)
        elif k == 4:
            nonlinear(w, h)
        elif k == 5:
            gather_forward(w, h, 0)
        elif k == 6:
            gather_end(w, h, 0)
            gather_start(w, h, 1)
        elif k == 7:
            gather_forward(w, h, 1)
        else:
            results(w)

    for item in ORDER:
        if len(item) == 1:
            pump(item[0])
        else:
            stage(*item)

    rows_x = X[...].reshape(512, 256)
    rows_g = GD[...].reshape(512, 256)
    stores = []
    for t, (n_h, rhs) in enumerate(((1, rows_x), (2, rows_x), (0, rows_g))):
        for n in range(6):
            cols = H3[n_h, :, n * 256 : (n + 1) * 256]
            OUT[t, n * 256 : (n + 1) * 256, :] = dot_first(cols, rhs).astype(BF)
        store = pltpu.make_async_copy(OUT.at[t], grads_out.at[t], o_sem.at[t])
        store.start()
        stores.append(store)

    s_i = lax.broadcasted_iota(jnp.int32, (128, 512), 1)
    l_i = lax.broadcasted_iota(jnp.int32, (128, 512), 0)

    def expert_of(s):
        blk = s // 16
        core = jnp.where(blk < NZ, c, 1 - c)
        return (z + blk % NZ) % NZ * 2 + core

    e_s = expert_of(s_i)
    pick_code = jnp.where(l_i == e_s, 1.0, 0.0).astype(BF)
    pick_w = jnp.where((l_i >= 32) & (l_i % 32 == e_s), 1.0, 0.0).astype(BF)
    own = G[0, 0, :, 512:640]
    code_s = dot_plain(own, pick_code)
    w_s = dot_plain(own, pick_w)
    s32 = lax.broadcasted_iota(jnp.int32, (32, 512), 1)
    chosen = code_s == (s32 % 16 + 1).astype(F32)
    weights = jnp.where(chosen, w_s, 0.0)
    w_hi = weights.astype(BF)
    w_lo = (weights - w_hi.astype(F32)).astype(BF)
    e32 = expert_of(s32)
    by_k = jnp.concatenate(
        [jnp.where(chosen & (e32.astype(F32) == ids_c[:, k : k + 1]), 1.0, 0.0) for k in range(8)], axis=0
    ).astype(BF)
    for copy in sent:
        copy.wait_send()
    for copy in back.values():
        copy.wait_recv()
    back_eo = RR[:, :, :, 0:256].reshape(512, 256)
    back_bo = RR[:, :, :, 256:512].reshape(512, 256)
    lo_out[...] = (dot_plain(w_hi, back_eo) + dot_plain(w_lo, back_eo)).astype(BF)
    tg_out[...] = dot_plain(jnp.where(chosen, 1.0, 0.0).astype(BF), back_bo).astype(BF)
    rg_b = RRG[...].reshape(32, 128)
    rg_hi = rg_b.astype(BF)
    rg_lo = (rg_b - rg_hi.astype(F32)).astype(BF)
    spread = jnp.where(l_i == s_i % 16, 1.0, 0.0).astype(BF)
    block = lax.broadcasted_iota(jnp.int32, (32, 512), 0) == s32 // 16
    rows2 = [
        jnp.sum(jnp.where(block, dot_plain(v, spread), 0.0), axis=0, keepdims=True)
        for v in (rg_hi, rg_lo)
    ]
    first_row = lax.broadcasted_iota(jnp.int32, (16, 512), 0) == 0
    both = dot_last(jnp.where(first_row, rows2[0], rows2[1]).astype(BF), by_k)
    both = both[0:1] + both[1:2]
    for k in range(8):
        rg_out[k : k + 1, :] = both[:, 32 * k : 32 * k + 32]

    for store in stores:
        store.wait()


def copy_out(lo, tg, rg, grads, lo_out, tg_out, rg_out, gg, ug, dg, LO, TG, RG, B, i_sem, o_sem):
    pairs = [(lo, LO, lo_out), (tg, TG, tg_out), (rg, RG, rg_out)]
    for t, dst in enumerate((gg, ug, dg)):
        for n in (0, 1):
            at = pl.ds(768 * n, 768)
            pairs.append((grads.at[t, at], B.at[t, at], dst.at[at]))
    ins = [pltpu.make_async_copy(a, b, i_sem.at[n]) for n, (a, b, _) in enumerate(pairs)]
    outs = [pltpu.make_async_copy(b, c, o_sem.at[n]) for n, (_, b, c) in enumerate(pairs)]
    for copy in ins:
        copy.start()
    for n in range(len(pairs)):
        ins[n].wait()
        outs[n].start()
    for copy in outs:
        copy.wait()


def local(tokens, expert_ids, route_weights, gate_weight, up_weight, down_weight, output_grad):
    vmem = pl.BlockSpec(memory_space=pltpu.VMEM)
    hbm = pl.BlockSpec(memory_space=pl.ANY)
    wshape = jax.ShapeDtypeStruct((1536, 256), BF)
    small = (
        jax.ShapeDtypeStruct((32, 256), BF),
        jax.ShapeDtypeStruct((32, 256), BF),
        jax.ShapeDtypeStruct((8, 32), F32),
    )
    dma = pltpu.SemaphoreType.DMA
    results = pl.pallas_call(
        kernel,
        out_shape=small + (jax.ShapeDtypeStruct((3, 1536, 256), BF),),
        in_specs=[vmem, vmem, vmem, vmem, hbm, hbm, hbm],
        out_specs=[vmem, vmem, vmem, hbm],
        scratch_shapes=[
            pltpu.VMEM((3, 1536, 256), BF),
            pltpu.VMEM((2, NZ, 32, 640), BF),
            pltpu.VMEM((NW, 128, 256), BF),
            pltpu.VMEM((NW, 128, 256), BF),
            pltpu.VMEM((NW, 8, 16, 128), F32),
            pltpu.VMEM((NW, 2, 4, 4, 9, 16, 128), BF),
            pltpu.VMEM((NW, 2, 4, 5, 16, 128), BF),
            pltpu.VMEM((NW, 2, 4, 4, 16, 128), BF),
            pltpu.VMEM((NW, 2, 4, 9, 16, 128), BF),
            pltpu.VMEM((NW, 2, 4, 9, 16, 128), BF),
            pltpu.VMEM((NW, 2, 5, 16, 128), BF),
            pltpu.VMEM((NW, 2, 4, 16, 128), BF),
            pltpu.VMEM((NW, 2, 9, 16, 128), BF),
            pltpu.VMEM((NW, 2, 9, 16, 128), BF),
            pltpu.VMEM((NW, 2, 4, 4, 10, 16, 128), BF),
            pltpu.VMEM((3, 512, 1536), BF),
            pltpu.VMEM((NW, 8, 16, 512), BF),
            pltpu.VMEM((2, NZ, 16, 512), BF),
            pltpu.VMEM((NW, 8, 1, 128), F32),
            pltpu.VMEM((2, NZ, 1, 128), F32),
            pltpu.VMEM((3, 1536, 256), BF),
            dma((3,)),
            dma((3,)),
            dma((4,)),
            dma((4,)),
            dma((2, 4)),
            dma((2, 4)),
            dma((9,)),
            dma((9,)),
            dma((NW, 2, 2, 2, 3)),
            dma((NW, 2, 2, 2, 3)),
            dma((NW, 2, 2, 2, 3)),
            dma((NW, 2, 2, 2, 3)),
            dma((2, NZ)),
            dma((2, NZ)),
            dma((2, NZ)),
            dma((2, NZ)),
        ],
        compiler_params=pltpu.CompilerParams(
            collective_id=0, has_side_effects=True, vmem_limit_bytes=60 * 1024 * 1024
        ),
        name="experts",
    )(
        tokens, expert_ids.T, route_weights.T, output_grad,
        gate_weight[0], up_weight[0], down_weight[0],
    )
    lo, tg, rg, gg, ug, dg = pl.pallas_call(
        copy_out,
        out_shape=small + (wshape, wshape, wshape),
        in_specs=[hbm] * 4,
        out_specs=[hbm] * 6,
        scratch_shapes=[
            pltpu.VMEM((32, 256), BF),
            pltpu.VMEM((32, 256), BF),
            pltpu.VMEM((8, 32), F32),
            pltpu.VMEM((3, 1536, 256), BF),
            dma((9,)),
            dma((9,)),
        ],
        name="copy_out",
    )(*results)
    return lo, tg, rg.T, gg[None], ug[None], dg[None]


def solution(mesh):
    placed = (
        P("expert", "dp"),
        P("expert", None),
        P("expert", None),
        P("expert", None, "dp"),
        P("expert", None, "dp"),
        P("expert", None, "dp"),
        P("expert", "dp"),
    )
    return jax.shard_map(
        local,
        mesh=mesh,
        in_specs=placed,
        out_specs=(
            P("expert", "dp"),
            P("expert", "dp"),
            P("expert", None),
            P("expert", None, "dp"),
            P("expert", None, "dp"),
            P("expert", None, "dp"),
        ),
        check_vma=False,
    )
```
